32 devices in a mesh: group: 2 (over x), cand: 16 (over z, y, core).
Axes of the slice: x: 2, y: 2, z: 4, core: 2. Of those that a mesh axis runs over, the one named last changes fastest.
Arguments:
- embeddings: bfloat16 [64, 1024, 768], P(('group', 'cand')), parts along dimension 0
- lengths: int32 [64], P(('group', 'cand')), parts along dimension 0, may hold values from 256 to 1024, as said below
Outputs:
- consensus: float32 [64, 1024], P(('group', 'cand')), parts along dimension 0
The draws below stay inside these ranges and needn't reach their ends.
There are 2 independent parts, one for each index of `group`. The reference program is written for one: setup_inputs(seed, part) draws one part's arguments, and reference() takes and returns one part's arrays. A program takes and returns all parts, laid end to end along the dimension named above; each array names one. Nothing has to cross between parts.
Inputs may be any that keep to these rules, and one draw needn't show every extreme that they name: `lengths`: at least one answer of every prompt has exactly 1024 tokens; every answer has 256 tokens or more.
All inputs are finite; a program needn't handle non-finite values.
Results may differ from the reference program's by a relative error of at most 0.0005.
Values may be sent and summed in bfloat16 or wider, within the bound.
A program may use at most 64 MiB of HBM per device.

```python
import jax
import jax.numpy as jnp
from jax import lax

A_DEV = 2
L = 1024
E = 768
ROUNDS = 2
CAND = 32
PARTNERS = 9
N_CAND = 16


def draw_embeddings(key, part):
    key_base = jax.random.fold_in(key, 11)
    base = jax.random.normal(key_base, (CAND, L, E), jnp.float32)
    return base.astype(jnp.bfloat16)


def draw_lengths(key, part):
    drawn = jax.random.randint(jax.random.fold_in(key, 21), (CAND,), L // 4, L + 1)
    where_full = jax.random.randint(jax.random.fold_in(key, 22), (), 0, CAND)
    return drawn.at[where_full].set(L).astype(jnp.int32)


def setup_inputs(seed: int = 0, part: int = 0) -> dict:
    streams_of = jax.random.split(jax.random.key(seed), 3)
    own_keys = jax.random.split(jax.random.fold_in(streams_of[2], part), 3)
    return {
        "embeddings": draw_embeddings(jax.random.fold_in(jax.random.fold_in(streams_of[2], part), 71), part),
        "lengths": draw_lengths(jax.random.fold_in(jax.random.fold_in(streams_of[2], part), 71), part),
    }


INV_TEMP = 256.0

def unit_rows(embeddings):
    values = embeddings.astype(jnp.float32)
    scale = lax.rsqrt(lax.optimization_barrier(jnp.sum(values * values, axis=-1, keepdims=True)) + 1e-06)
    return (values * scale).astype(jnp.bfloat16)

def soft_terms(left, left_valid, right, right_valid):
    scores = jnp.einsum('te,bse->bts', left.astype(jnp.float32), right.astype(jnp.float32)) * INV_TEMP
    row_scores = jnp.where(right_valid[:, None, :] > 0.5, scores, -1e+30)
    row_peak = lax.optimization_barrier(jnp.max(row_scores, axis=2, keepdims=True))
    row_terms = (row_peak[..., 0] + jnp.log(lax.optimization_barrier(jnp.sum(jnp.exp(row_scores - row_peak), axis=2)))) / INV_TEMP
    col_scores = jnp.where(left_valid[None, :, None] > 0.5, scores, -1e+30)
    col_peak = lax.optimization_barrier(jnp.max(col_scores, axis=1, keepdims=True))
    col_terms = (col_peak[:, 0, :] + jnp.log(lax.optimization_barrier(jnp.sum(jnp.exp(col_scores - col_peak), axis=1)))) / INV_TEMP
    return (row_terms, col_terms)

def reference(embeddings, lengths):
    unit = unit_rows(embeddings)
    valid = (jnp.arange(L, dtype=jnp.int32)[None, :] < lengths[:, None]).astype(jnp.float32)

    def visit(totals, index):
        block = index // A_DEV
        start = (block * A_DEV).astype(jnp.int32)
        mine = unit[index]
        mine_valid = valid[index]
        same = lax.dynamic_slice_in_dim(unit, start, A_DEV, 0)
        same_valid = lax.dynamic_slice_in_dim(valid, start, A_DEV, 0)
        row_terms, unused = soft_terms(mine, mine_valid, same, same_valid)
        weight = (jnp.arange(A_DEV, dtype=jnp.int32) + start != index).astype(jnp.float32)
        own_sum = lax.optimization_barrier(jnp.sum(row_terms * weight[:, None], axis=0))
        for offset in range(1, ROUNDS + 1):
            other = ((block - offset) % N_CAND * A_DEV).astype(jnp.int32)
            theirs = lax.dynamic_slice_in_dim(unit, other, A_DEV, 0)
            their_valid = lax.dynamic_slice_in_dim(valid, other, A_DEV, 0)
            row_terms, col_terms = soft_terms(mine, mine_valid, theirs, their_valid)
            own_sum = own_sum + lax.optimization_barrier(jnp.sum(row_terms, axis=0))
            current = lax.dynamic_slice_in_dim(totals, other, A_DEV, 0)
            totals = lax.dynamic_update_slice_in_dim(totals, current + col_terms, other, 0)
        totals = totals.at[index].add(own_sum)
        return (totals, None)
    totals, unused = lax.scan(visit, jnp.zeros((CAND, L), jnp.float32), jnp.arange(CAND, dtype=jnp.int32))
    return totals * valid / PARTNERS
```

```python
import functools
import math

import jax
import jax.numpy as jnp
from jax import lax
from jax.experimental import pallas as pl
from jax.experimental.pallas import tpu as pltpu
from jax.sharding import PartitionSpec as P

MESH = pl.DeviceIdType.MESH
SCALE = 256.0 * math.log2(math.e)
LOW = -1e30
PIECE = 128
ROWS = 256
WIDE = 256
DETOUR = (3, 3)
RING = (-4, -3, -2, -1, 1, 2, 3, 4)
LENS = (-3, -2, -1, 1, 2)


def unit_rows(raw):
    values = raw.astype(jnp.float32)
    scale = lax.rsqrt(jnp.sum(values * values, axis=-1, keepdims=True) + 1e-06)
    return (values * scale).astype(jnp.bfloat16)


def kernel(
    n, detour, x_hbm, lens_ref, out_ref,
    raw, units, far, relay, fresh, board_a, board_b, lens, bias, peak, mass, total, back,
    local_sem, near_sems, lens_send, lens_recv, send_sem, far_recv, pass_send, relay_recv, relay_send,
    back_send, back_recv,
):
    length = x_hbm.shape[1]
    chunks = length // PIECE
    per = ROWS // PIECE
    boards = (board_a, board_b)
    group = lax.axis_index("group")
    place = lax.axis_index("cand")
    twin = group + 1 - 2 * lax.rem(group, 2)
    flip = lax.rem(group, 2)
    me = place + flip * (n - 1 - 2 * place)
    role = lax.rem(me, 4)
    core = lax.rem(me, 2)
    partner = me + 1 - 2 * core
    even, odd = role < 2, role >= 2

    def spot(m):
        m = lax.rem(m + n, n)
        return m + flip * (n - 1 - 2 * m)

    def ring(m):
        return (group, spot(m))

    across = (twin, place)
    corner = (twin, spot(jnp.where(even, me + 2, me - 2)))

    for a in range(2):
        lens[0, a : a + 1] = jnp.full((1, 128), lens_ref[a], jnp.int32)

    barrier = pltpu.get_barrier_semaphore()
    meets = [ring(me + d) for d in RING]
    if sum(detour):
        meets += [across, corner]
    for device in meets:
        pl.semaphore_signal(barrier, inc=1, device_id=device, device_id_type=MESH)
    local = pltpu.make_async_copy(x_hbm, raw.at[0], local_sem)
    local.start()
    pl.semaphore_wait(barrier, len(meets))

    def remote(src, dst, send, recv, device):
        return pltpu.make_async_remote_copy(
            src_ref=src, dst_ref=dst, send_sem=send, recv_sem=recv,
            device_id=device, device_id_type=MESH,
        )

    def rows_of(k):
        return pl.ds(pl.multiple_of(k * PIECE, PIECE), PIECE)

    def spread(i):
        d = LENS[i]
        return remote(lens.at[0], lens.at[1 + i], lens_send.at[i], lens_recv.at[i], ring(me - d))

    near = remote(x_hbm, raw.at[1], near_sems.at[0], near_sems.at[1], ring(partner))

    def own_piece(a, k, slot, device):
        return remote(x_hbm.at[a, rows_of(k)], far.at[slot, rows_of(k)], send_sem.at[a, k], far_recv.at[slot, k], device)

    def around(a, k):
        return remote(x_hbm.at[a, rows_of(k)], relay.at[a, k], send_sem.at[a, k], relay_recv.at[a, k], corner)

    def bypass(a, k):
        return remote(relay.at[a, k], far.at[a, rows_of(k)], relay_send.at[a, k], far_recv.at[a, k], across)

    def detours(a, k):
        return k % 2 == 1 and k // 2 < detour[a]

    order = [(a, k) for k in range(chunks) for a in range(2)]
    for i in range(len(LENS)):
        spread(i).start()

    @pl.when(role == 3)
    def _():
        for a, k in order:
            if detours(a, k):
                around(a, k).start()
        for a, k in order:
            if not detours(a, k):
                own_piece(a, k, a, ring(me - 2)).start()

    @pl.when(role == 2)
    def _():
        for a, k in order:
            own_piece(a, k, a, ring(me - 2)).start()

    @pl.when(role == 0)
    def _():
        for a, k in order:
            own_piece(a, k, 0, ring(me + 2 + a)).start()

    @pl.when(role != 0)
    def _():
        near.start()

    lane = lax.broadcasted_iota(jnp.int32, (1, length), 1)
    row = lax.broadcasted_iota(jnp.int32, (PIECE, 128), 0)
    eye = lax.broadcasted_iota(jnp.int32, (PIECE, PIECE), 0) == lax.broadcasted_iota(
        jnp.int32, (PIECE, PIECE), 1
    )
    total[...] = jnp.zeros_like(total)
    peak[...] = jnp.full_like(peak, LOW)
    mass[...] = jnp.zeros_like(mass)

    def set_bias(slot, counts):
        for a in range(2):
            bias[slot + a] = jnp.where(lane < counts[a : a + 1, 0:1], 0.0, LOW)

    def normalise(slot):
        def one(i, carry):
            a, k = i // chunks, lax.rem(i, chunks)
            units[2 * slot + a, rows_of(k)] = unit_rows(raw[slot, a, rows_of(k)])
            return carry

        lax.fori_loop(0, 2 * chunks, one, 0)

    def unit(query, left, count, halves):
        for a in range(count):
            for j in range(0, length, WIDE):
                boards[a][:, j : j + WIDE] = lax.dot_general(
                    query, units[left + a, j : j + WIDE], (((1,), (1,)), ((), ())),
                    preferred_element_type=jnp.float32,
                )
        for h, (counts, first, pair, slot) in enumerate(halves):
            part = slice(h * PIECE, (h + 1) * PIECE)
            row_bias = jnp.where(row + first < counts, 0.0, LOW)
            term = None
            for a in range(count):
                value = soften(boards[a], part, left + a, pair + a, row_bias)
                term = value if term is None else term + value
            cols = pl.ds(pl.multiple_of(first, PIECE), PIECE)
            total[slot, :, cols] = total[slot, :, cols] + jnp.sum(
                jnp.where(eye, jnp.broadcast_to(term, (PIECE, PIECE)), 0.0), axis=0, keepdims=True
            )

    def soften(board, part, left, pair, row_bias):
        tops = None
        for j in range(0, length, 128):
            cols = slice(j, j + 128)
            scores = board[part, cols] * SCALE + bias[left, :, cols] + row_bias
            board[part, cols] = scores
            tops = scores if tops is None else jnp.maximum(tops, scores)
            before = peak[pair, :, cols]
            now = jnp.maximum(before, jnp.max(scores, axis=0, keepdims=True))
            peak[pair, :, cols] = now
            mass[pair, :, cols] = mass[pair, :, cols] * jnp.exp2(before - now)
        top = jnp.max(tops, axis=1, keepdims=True)
        wide = jnp.broadcast_to(top, (PIECE, 128))
        sums = None
        for j in range(0, length, 128):
            cols = slice(j, j + 128)
            scores = board[part, cols]
            value = jnp.exp2(scores - wide)
            sums = value if sums is None else sums + value
            value = jnp.exp2(scores - peak[pair, :, cols])
            mass[pair, :, cols] = mass[pair, :, cols] + jnp.sum(value, axis=0, keepdims=True)
        return top + jnp.log2(jnp.sum(sums, axis=1, keepdims=True))

    def close(slot, pair):
        total[slot] = total[slot] + peak[pair] + jnp.log2(mass[pair])

    local.wait()
    set_bias(0, lens[0])
    normalise(0)
    for i in range(len(LENS)):
        spread(i).wait()

    @pl.when(role != 1)
    def _():
        near.wait_recv()
        set_bias(2, lens[1 + LENS.index(1)])
        normalise(1)

    @pl.when((role == 1) | (role == 3))
    def _():
        set_bias(2, lens[1 + LENS.index(-1)])

    def lens_at(d, a):
        return lens[1 + LENS.index(d), a : a + 1]

    base = jnp.where((role == 0) | (role == 3), 2, 0)
    last = jnp.where(role >= 2, 2 - base, base)

    def arrive(slot, k):
        remote(x_hbm.at[0, rows_of(k)], far.at[slot, rows_of(k)], pass_send.at[0, 0], far_recv.at[slot, k], across).wait_recv()

    def passing(slot, k):
        target = jnp.where(even, me + 4, me - 4)
        there = jnp.where(even, slot + 2, slot + 1)
        return remote(far.at[slot, rows_of(k)], far.at[there, rows_of(k)], pass_send.at[slot, k], far_recv.at[there, k], ring(target))

    def hand_on(slot, k):
        arrive(slot, k)
        passing(slot, k).start()

    def tile_rows(tile):
        return pl.ds(pl.multiple_of(tile * ROWS, ROWS), ROWS)

    def take_local(slot, k, stage, h):
        fresh[stage, h * PIECE : (h + 1) * PIECE] = units[slot, rows_of(k)]

    def take_far(slot, k, stage, h):
        fresh[stage, h * PIECE : (h + 1) * PIECE] = unit_rows(far[slot, rows_of(k)])

    counts = [None] * 4
    own_len = [lens[0, a : a + 1] for a in range(2)]
    is0, is1, is2, is3 = (jnp.full((1, 128), role, jnp.int32) == r for r in range(4))
    pick = lambda v0, v1, v2, v3: jnp.where(is0, v0, jnp.where(is1, v1, jnp.where(is2, v2, v3)))
    counts[0] = pick(own_len[0], lens_at(2, 0), lens_at(1, 0), own_len[1])
    counts[1] = pick(own_len[1], lens_at(2, 1), lens_at(-2, 0), lens_at(-3, 1))
    counts[2] = pick(lens_at(2, 0), lens_at(-2, 0), lens_at(2, 0), lens_at(1, 1))
    counts[3] = pick(lens_at(2, 1), lens_at(-2, 1), lens_at(2, 0), lens_at(1, 1))
    choose = lambda v0, v1, v2, v3: jnp.where(role == 0, v0, jnp.where(role == 1, v1, jnp.where(role == 2, v2, v3)))
    slots = [choose(0, 4, 2, 1), choose(1, 5, 4, 4), choose(4, 6, 5, 5), choose(5, 7, 5, 5)]

    routed = [(a, k) for a, k in order if detours(a, k)]

    def step(j, carry):
        @pl.when(j < chunks)
        def _():
            @pl.when(role == 1)
            def _():
                hand_on(0, j)
                take_far(0, j, 0, 0)

            @pl.when(role != 1)
            def _():
                take_local(choose(0, 0, 2, 1), j, 0, 0)

            @pl.when(role == 2)
            def _():
                for i, (a, k) in enumerate(routed):
                    @pl.when(j == i * chunks // len(routed))
                    def _():
                        around(a, k).wait_recv()
                        bypass(a, k).start()

            @pl.when(role == 0)
            def _():
                take_local(1, j, 0, 1)

            @pl.when(role != 0)
            def _():
                slot = jnp.where(role == 1, 1, 0)
                hand_on(slot, j)
                take_far(slot, j, 0, 1)

            unit(fresh[0], base, 2, [(counts[0], j * PIECE, 0, slots[0]), (counts[1], j * PIECE, 2, slots[1])])

            @pl.when(lax.rem(j, per) == 0)
            def _():
                unit(units[1, tile_rows(j // per)], 0, 1, [(own_len[1], (j + h) * PIECE, 8, 1) for h in range(per)])

        @pl.when(j >= per)
        def _():
            k = j - per
            late = lax.rem(j, per)

            @pl.when(even)
            def _():
                for h in range(2):
                    slot = choose(h, 2 + h, 0, 0)
                    arrive(slot, k)
                    take_far(slot, k, 1, h)

            @pl.when(odd & (late == 0))
            def _():
                for h in range(per):
                    arrive(1, k + h)
                    take_far(1, k + h, 1, h)

            left = jnp.where(late == 0, base, last)
            unit(
                fresh[1], left, 2,
                [
                    (counts[2], jnp.where(even, k, k - late) * PIECE, jnp.where(even, 4, 4 + 2 * late), slots[2]),
                    (counts[3], jnp.where(even, k, k - late + 1) * PIECE, jnp.where(even, 6, 4 + 2 * late), slots[3]),
                ],
            )

        return carry

    lax.fori_loop(0, chunks + per, step, 0)

    close(0, 8)
    for s in range(4):
        left = last if s == 3 else base
        for a in range(2):
            close(left + a, 2 * s + a)

    def give(src, dst, device):
        return remote(total.at[src], back.at[dst], back_send.at[src], back_recv.at[dst], device)

    gives = (
        [give(2, 0, ring(partner)), give(3, 1, ring(partner)), give(4, 2, ring(me + 2)), give(5, 3, ring(me + 2))],
        [give(4, 2, ring(me + 2)), give(5, 3, ring(me + 2)), give(6, 4, ring(me - 2)), give(7, 5, ring(me - 2))],
        [give(2, 0, ring(partner)), give(3, 1, ring(partner)), give(4, 2, ring(me - 2)), give(5, 4, ring(me + 2))],
        [give(2, 0, ring(partner)), give(3, 1, ring(partner)), give(4, 3, ring(me - 3)), give(5, 5, ring(me + 1))],
    )
    takes = ([2, 3, 4, 5], [0, 1], [0, 1, 2, 3], [0, 1, 2, 3, 4, 5])
    for r in range(4):
        @pl.when(role == r)
        def _():
            for copy in gives[r]:
                copy.start()
            for copy in gives[r]:
                copy.wait_send()
            for b in takes[r]:
                give(0, b, ring(partner)).wait_recv()
            for a in range(2):
                whole = total[a]
                for b in takes[r]:
                    if b % 2 == a:
                        whole = whole + back[b]
                out_ref[a : a + 1] = jnp.where(bias[a] == 0.0, whole, 0.0)

    @pl.when(role != 0)
    def _():
        near.wait_send()

    @pl.when(role != 1)
    def _():
        for a, k in order:
            own_piece(a, k, a, ring(partner)).wait_send()

    @pl.when(role == 1)
    def _():
        for a, k in order:
            passing(a, k).wait_send()

    @pl.when(odd)
    def _():
        for k in range(chunks):
            passing(0, k).wait_send()

    @pl.when(role == 2)
    def _():
        for a, k in routed:
            bypass(a, k).wait_send()


def solution(mesh):
    n = mesh.shape["cand"]
    detour = DETOUR if mesh.shape["group"] % 2 == 0 else (0, 0)

    def shards(embeddings, lengths):
        answers, length, width = embeddings.shape
        chunks = length // PIECE
        dma = pltpu.SemaphoreType.DMA
        sums = pl.pallas_call(
            functools.partial(kernel, n, detour),
            out_shape=jax.ShapeDtypeStruct((answers, length), jnp.float32),
            in_specs=[
                pl.BlockSpec(memory_space=pl.ANY),
                pl.BlockSpec(memory_space=pltpu.SMEM),
            ],
            out_specs=pl.BlockSpec(memory_space=pltpu.VMEM),
            scratch_shapes=[
                pltpu.VMEM((2, answers, length, width), jnp.bfloat16),
                pltpu.VMEM((4, length, width), jnp.bfloat16),
                pltpu.VMEM((4, length, width), jnp.bfloat16),
                pltpu.VMEM((2, chunks, PIECE, width), jnp.bfloat16),
                pltpu.VMEM((2, ROWS, width), jnp.bfloat16),
                pltpu.VMEM((ROWS, length), jnp.float32),
                pltpu.VMEM((ROWS, length), jnp.float32),
                pltpu.VMEM((1 + len(LENS), answers, 128), jnp.int32),
                pltpu.VMEM((4, 1, length), jnp.float32),
                pltpu.VMEM((9, 1, length), jnp.float32),
                pltpu.VMEM((9, 1, length), jnp.float32),
                pltpu.VMEM((8, 1, length), jnp.float32),
                pltpu.VMEM((6, 1, length), jnp.float32),
                dma, dma((2,)), dma((len(LENS),)), dma((len(LENS),)),
                dma((2, chunks)), dma((4, chunks)), dma((2, chunks)),
                dma((2, chunks)), dma((2, chunks)), dma((8,)), dma((6,)),
            ],
            compiler_params=pltpu.CompilerParams(collective_id=0, has_side_effects=True),
            name="consensus",
        )(embeddings, lengths)
        return sums * (math.log(2.0) / (256.0 * (answers - 1 + 4 * answers)))

    return jax.shard_map(
        shards,
        mesh=mesh,
        in_specs=(P(("group", "cand"), None, None), P(("group", "cand"))),
        out_specs=P(("group", "cand"), None),
        check_vma=False,
    )
```

```python
import functools
import math

import jax
import jax.numpy as jnp
from jax import lax
from jax.experimental import pallas as pl
from jax.experimental.pallas import tpu as pltpu
from jax.sharding import PartitionSpec as P

MESH = pl.DeviceIdType.MESH
SCALE = 256.0 * math.log2(math.e)
LOW = -1e30
PIECE = 128
ROWS = 256
WIDE = 256
DETOUR = (3, 3)
PACE = (0, 2, 2, 2, 0, 0, 0, 0)
TURN = 1


def unit_rows(raw):
    values = raw.astype(jnp.float32)
    scale = lax.rsqrt(jnp.sum(values * values, axis=-1, keepdims=True) + 1e-06)
    return (values * scale).astype(jnp.bfloat16)


def kernel(
    n, detour, x_hbm, lens_ref, out_ref,
    raw, units, far, relay, fresh, board_a, board_b, lens, bias, peak, mass, total, back,
    local_sem, near_sems, lens_send, lens_recv, send_sem, far_recv, pass_send, turn_send, relay_recv, relay_send,
    back_send, back_recv, up_sem, down_sem,
):
    length = x_hbm.shape[1]
    chunks = length // PIECE
    per = ROWS // PIECE
    boards = (board_a, board_b)
    group = lax.axis_index("group")
    place = lax.axis_index("cand")
    twin = group + 1 - 2 * lax.rem(group, 2)
    flip = lax.rem(group, 2)
    me = place + flip * (n - 1 - 2 * place)
    role = lax.rem(me, 4)
    core = lax.rem(me, 2)
    partner = me + 1 - 2 * core
    even, odd = role < 2, role >= 2

    def spot(m):
        m = lax.rem(m + n, n)
        return m + flip * (n - 1 - 2 * m)

    def ring(m):
        return (group, spot(m))

    across = (twin, place)
    corner = (twin, spot(jnp.where(even, me + 2, me - 2)))

    for a in range(2):
        lens[0, a : a + 1] = jnp.full((1, 128), lens_ref[a], jnp.int32)

    barrier = pltpu.get_barrier_semaphore()
    quad, quads = me // 4, n // 4
    below, above = quad > 0, quad < quads - 1
    meets = [ring(me - role + lax.rem(role + i, 4)) for i in range(1, 4)] + [across, corner]
    for device in meets:
        pl.semaphore_signal(barrier, inc=1, device_id=device, device_id_type=MESH)

    @pl.when(below)
    def _():
        pl.semaphore_signal(barrier, inc=1, device_id=ring(me - 4), device_id_type=MESH)

    @pl.when(above)
    def _():
        pl.semaphore_signal(barrier, inc=1, device_id=ring(me + 4), device_id_type=MESH)

    local = pltpu.make_async_copy(x_hbm, raw.at[0], local_sem)
    local.start()
    pl.semaphore_wait(barrier, len(meets) + below.astype(jnp.int32) + above.astype(jnp.int32))

    def rise():
        @pl.when(below)
        def _():
            pl.semaphore_wait(up_sem, 1)

        @pl.when(above)
        def _():
            pl.semaphore_signal(up_sem, inc=1, device_id=ring(me + 4), device_id_type=MESH)

    def fall():
        @pl.when(above)
        def _():
            pl.semaphore_wait(down_sem, 1)

        @pl.when(below)
        def _():
            pl.semaphore_signal(down_sem, inc=1, device_id=ring(me - 4), device_id_type=MESH)

    def remote(src, dst, send, recv, device):
        return pltpu.make_async_remote_copy(
            src_ref=src, dst_ref=dst, send_sem=send, recv_sem=recv,
            device_id=device, device_id_type=MESH,
        )

    def rows_of(k):
        return pl.ds(pl.multiple_of(k * PIECE, PIECE), PIECE)

    def spread(i, slot, device):
        return remote(lens.at[0], lens.at[slot], lens_send.at[i], lens_recv.at[slot], device)

    def further():
        target = jnp.where(even, me + 4, me - 4)
        return remote(lens.at[2], lens.at[3], lens_send.at[3], lens_recv.at[3], ring(target))

    def meet_far():
        @pl.when(2 * quad < quads)
        def _():
            rise()
            fall()

        @pl.when(2 * quad >= quads)
        def _():
            fall()
            rise()

    near = remote(x_hbm, raw.at[1], near_sems.at[0], near_sems.at[1], ring(partner))

    def piece(src, a, k, slot, device):
        return remote(src.at[a, rows_of(k)], far.at[slot, rows_of(k)], send_sem.at[a, k], far_recv.at[slot, k], device)

    def around(a, k):
        return remote(x_hbm.at[a, rows_of(k)], relay.at[a, k], turn_send.at[a, k], relay_recv.at[a, k], corner)

    def bypass(a, k):
        return remote(relay.at[a, k], far.at[a, rows_of(k)], relay_send.at[a, k], far_recv.at[a, k], across)

    routed = [(a, k) for k in range(chunks) for a in range(2) if k < detour[a]]
    starts = [min(sum(PACE[:i]), len(routed)) for i in range(len(PACE))] + [len(routed)]
    direct = [[k for k in range(chunks) if (a, k) not in routed] for a in range(2)]

    spread(0, 1, ring(partner)).start()

    @pl.when(odd)
    def _():
        spread(1, 2, ring(me - 2)).start()

    @pl.when(role == 0)
    def _():
        spread(1, 2, ring(me + 2)).start()
        spread(2, 2, ring(me + 3)).start()

    @pl.when(role != 0)
    def _():
        near.start()

    @pl.when(role == 0)
    def _():
        for k in range(chunks):
            for a in range(2):
                piece(x_hbm, a, k, 0, ring(me + 2 + a)).start()

    @pl.when(role == 3)
    def _():
        for k in range(chunks):
            piece(x_hbm, 0, k, 0, ring(me - 2)).start()

    @pl.when(odd)
    def _():
        near.wait_recv()

    @pl.when(role == 2)
    def _():
        for k in range(chunks):
            piece(raw.at[1], 1, k, 1, ring(me - 1)).start()
        for k in direct[0]:
            piece(x_hbm, 0, k, 0, ring(me - 2)).start()

    @pl.when(role == 3)
    def _():
        for k in direct[1]:
            piece(raw.at[1], 1, k, 1, ring(me - 3)).start()

    meet_far()
    lane = lax.broadcasted_iota(jnp.int32, (1, length), 1)
    row = lax.broadcasted_iota(jnp.int32, (PIECE, 128), 0)
    eye = lax.broadcasted_iota(jnp.int32, (PIECE, PIECE), 0) == lax.broadcasted_iota(
        jnp.int32, (PIECE, PIECE), 1
    )
    total[...] = jnp.zeros_like(total)
    peak[...] = jnp.full_like(peak, LOW)
    mass[...] = jnp.zeros_like(mass)

    def set_bias(slot, counts):
        for a in range(2):
            bias[slot + a] = jnp.where(lane < counts[a : a + 1, 0:1], 0.0, LOW)

    def normalise(slot):
        def one(i, carry):
            a, k = i // chunks, lax.rem(i, chunks)
            units[2 * slot + a, rows_of(k)] = unit_rows(raw[slot, a, rows_of(k)])
            return carry

        lax.fori_loop(0, 2 * chunks, one, 0)

    def unit(query, left, count, halves):
        for a in range(count):
            for j in range(0, length, WIDE):
                boards[a][:, j : j + WIDE] = lax.dot_general(
                    query, units[left + a, j : j + WIDE], (((1,), (1,)), ((), ())),
                    preferred_element_type=jnp.float32,
                )
        for h, (counts, first, pair, slot) in enumerate(halves):
            part = slice(h * PIECE, (h + 1) * PIECE)
            row_bias = jnp.where(row + first < counts, 0.0, LOW)
            term = None
            for a in range(count):
                value = soften(boards[a], part, left + a, pair + a, row_bias)
                term = value if term is None else term + value
            cols = pl.ds(pl.multiple_of(first, PIECE), PIECE)
            total[slot, :, cols] = total[slot, :, cols] + jnp.sum(
                jnp.where(eye, jnp.broadcast_to(term, (PIECE, PIECE)), 0.0), axis=0, keepdims=True
            )

    def soften(board, part, left, pair, row_bias):
        tops = None
        for j in range(0, length, 128):
            cols = slice(j, j + 128)
            scores = board[part, cols] * SCALE + bias[left, :, cols] + row_bias
            board[part, cols] = scores
            tops = scores if tops is None else jnp.maximum(tops, scores)
            before = peak[pair, :, cols]
            now = jnp.maximum(before, jnp.max(scores, axis=0, keepdims=True))
            peak[pair, :, cols] = now
            mass[pair, :, cols] = mass[pair, :, cols] * jnp.exp2(before - now)
        top = jnp.max(tops, axis=1, keepdims=True)
        wide = jnp.broadcast_to(top, (PIECE, 128))
        sums = None
        for j in range(0, length, 128):
            cols = slice(j, j + 128)
            scores = board[part, cols]
            value = jnp.exp2(scores - wide)
            sums = value if sums is None else sums + value
            value = jnp.exp2(scores - peak[pair, :, cols])
            mass[pair, :, cols] = mass[pair, :, cols] + jnp.sum(value, axis=0, keepdims=True)
        return top + jnp.log2(jnp.sum(sums, axis=1, keepdims=True))

    def close(slot, pair):
        total[slot] = total[slot] + peak[pair] + jnp.log2(mass[pair])

    local.wait()
    set_bias(0, lens[0])
    normalise(0)
    spread(0, 1, ring(partner)).wait_recv()
    spread(1, 2, ring(partner)).wait_recv()

    @pl.when(role != 0)
    def _():
        further().start()

    @pl.when(role == 0)
    def _():
        near.wait_recv()

    @pl.when(role != 1)
    def _():
        set_bias(2, lens[1])
        normalise(1)

    base = jnp.where((role == 0) | (role == 3), 2, 0)
    last = jnp.where(role >= 2, 2 - base, base)

    def arrive(slot, k):
        remote(x_hbm.at[0, rows_of(k)], far.at[slot, rows_of(k)], pass_send.at[0, 0], far_recv.at[slot, k], across).wait_recv()

    def passing(slot, k):
        target = jnp.where(even, me + 4, me - 4)
        there = jnp.where(even, slot + 2, slot + 1)
        return remote(far.at[slot, rows_of(k)], far.at[there, rows_of(k)], pass_send.at[slot, k], far_recv.at[there, k], ring(target))

    def hand_on(slot, k):
        arrive(slot, k)
        passing(slot, k).start()

    def tile_rows(tile):
        return pl.ds(pl.multiple_of(tile * ROWS, ROWS), ROWS)

    def take_local(slot, k, stage, h):
        fresh[stage, h * PIECE : (h + 1) * PIECE] = units[slot, rows_of(k)]

    def take_far(slot, k, stage, h):
        fresh[stage, h * PIECE : (h + 1) * PIECE] = unit_rows(far[slot, rows_of(k)])

    own_len = [lens[0, a : a + 1] for a in range(2)]
    is0, is1, is2, is3 = (jnp.full((1, 128), role, jnp.int32) == r for r in range(4))
    pick = lambda v0, v1, v2, v3: jnp.where(is0, v0, jnp.where(is1, v1, jnp.where(is2, v2, v3)))

    def lens_at(slot, a):
        return lens[slot, a : a + 1]

    def soon():
        return (
            pick(own_len[0], lens_at(2, 0), lens_at(1, 0), own_len[1]),
            pick(own_len[1], lens_at(2, 1), lens_at(2, 0), lens_at(2, 1)),
        )

    def later():
        return (
            pick(lens_at(2, 0), lens_at(3, 0), lens_at(3, 0), lens_at(3, 1)),
            pick(lens_at(2, 1), lens_at(3, 1), lens_at(3, 0), lens_at(3, 1)),
        )

    choose = lambda v0, v1, v2, v3: jnp.where(role == 0, v0, jnp.where(role == 1, v1, jnp.where(role == 2, v2, v3)))
    slots = [choose(0, 4, 2, 1), choose(1, 5, 4, 4), choose(4, 6, 5, 5), choose(5, 7, 5, 5)]

    def routes(j, act):
        for i in range(len(PACE)):
            if starts[i] < starts[i + 1]:
                @pl.when(j == i)
                def _():
                    for a, k in routed[starts[i] : starts[i + 1]]:
                        act(a, k)

    def turn(a, k):
        around(a, k).wait_recv()
        bypass(a, k).start()

    lag = jnp.where(role == 0, chunks, per)

    def step(j, carry):
        @pl.when(role == 2)
        def _():
            routes(j, lambda a, k: around(a, k).start())

        @pl.when(j < chunks)
        def _():
            @pl.when(role == 1)
            def _():
                hand_on(0, j)
                take_far(0, j, 0, 0)

            @pl.when(role != 1)
            def _():
                take_local(choose(0, 0, 2, 1), j, 0, 0)

            @pl.when(role == 0)
            def _():
                take_local(1, j, 0, 1)

            @pl.when(role != 0)
            def _():
                slot = jnp.where(role == 1, 1, 0)
                hand_on(slot, j)
                take_far(slot, j, 0, 1)

            counts = soon()
            unit(fresh[0], base, 2, [(counts[0], j * PIECE, 0, slots[0]), (counts[1], j * PIECE, 2, slots[1])])

            @pl.when(lax.rem(j, per) == 0)
            def _():
                unit(units[1, tile_rows(j // per)], 0, 1, [(own_len[1], (j + h) * PIECE, 8, 1) for h in range(per)])

        @pl.when((j >= lag) & (j < lag + chunks))
        def _():
            k = j - lag
            late = lax.rem(k, per)

            @pl.when((j == lag) & (role != 0))
            def _():
                further().wait_recv()


            @pl.when(even)
            def _():
                for h in range(2):
                    slot = choose(h, 2 + h, 0, 0)
                    arrive(slot, k)
                    take_far(slot, k, 1, h)

            @pl.when(odd & (late == 0))
            def _():
                for h in range(per):
                    arrive(1, k + h)
                    take_far(1, k + h, 1, h)

            left = jnp.where(late == 0, base, last)
            counts = later()
            unit(
                fresh[1], left, 2,
                [
                    (counts[0], jnp.where(even, k, k - late) * PIECE, jnp.where(even, 4, 4 + 2 * late), slots[2]),
                    (counts[1], jnp.where(even, k, k - late + 1) * PIECE, jnp.where(even, 6, 4 + 2 * late), slots[3]),
                ],
            )

        @pl.when(role == 3)
        def _():
            routes(j - TURN, turn)

        return carry

    lax.fori_loop(0, 2 * chunks, step, 0)

    def give(src, dst, device):
        return remote(total.at[src], back.at[dst], back_send.at[src], back_recv.at[dst], device)

    gives = (
        [give(4, 2, ring(me + 2)), give(5, 3, ring(me + 2))],
        [give(6, 4, ring(me - 2)), give(7, 5, ring(me - 2)), give(4, 2, ring(me + 2)), give(5, 3, ring(me + 2))],
        [give(5, 4, ring(me + 2)), give(4, 2, ring(me - 2))],
        [give(5, 5, ring(me + 1)), give(4, 3, ring(me - 3))],
    )
    for r in range(4):
        @pl.when(role == r)
        def _():
            for copy in gives[r]:
                copy.start()

    close(0, 8)
    for s in range(4):
        left = last if s == 3 else base
        for a in range(2):
            close(left + a, 2 * s + a)

    @pl.when(role != 1)
    def _():
        for a in range(2):
            give(2 + a, a, ring(partner)).start()

    takes = ([2, 3, 4, 5], [0, 1], [0, 1, 2, 3], [0, 1, 2, 3, 4, 5])
    for r in range(4):
        @pl.when(role == r)
        def _():
            for b in takes[r]:
                give(0, b, ring(partner)).wait_recv()
            for a in range(2):
                whole = total[a]
                for b in takes[r]:
                    if b % 2 == a:
                        whole = whole + back[b]
                out_ref[a : a + 1] = jnp.where(bias[a] == 0.0, whole, 0.0)
            for copy in gives[r]:
                copy.wait_send()

    @pl.when(role != 1)
    def _():
        for a in range(2):
            give(2 + a, a, ring(partner)).wait_send()

    spread(0, 1, ring(partner)).wait_send()

    @pl.when(role != 1)
    def _():
        spread(1, 2, ring(partner)).wait_send()

    @pl.when(role == 0)
    def _():
        spread(2, 2, ring(partner)).wait_send()

    @pl.when(role != 0)
    def _():
        further().wait_send()

    @pl.when(role != 0)
    def _():
        near.wait_send()

    def sent(a, pieces):
        for k in pieces:
            piece(x_hbm, a, k, a, ring(partner)).wait_send()

    @pl.when(role == 0)
    def _():
        sent(0, range(chunks))
        sent(1, range(chunks))

    @pl.when(role == 2)
    def _():
        sent(1, range(chunks))
        sent(0, direct[0])
        for a, k in routed:
            around(a, k).wait_send()

    @pl.when(role == 3)
    def _():
        sent(0, range(chunks))
        sent(1, direct[1])

    @pl.when(role == 1)
    def _():
        for k in range(chunks):
            for a in range(2):
                passing(a, k).wait_send()

    @pl.when(odd)
    def _():
        for k in range(chunks):
            passing(0, k).wait_send()

    @pl.when(role == 3)
    def _():
        for a, k in routed:
            bypass(a, k).wait_send()


def solution(mesh):
    n = mesh.shape["cand"]
    detour = DETOUR if mesh.shape["group"] % 2 == 0 else (0, 0)

    def shards(embeddings, lengths):
        answers, length, width = embeddings.shape
        chunks = length // PIECE
        dma = pltpu.SemaphoreType.DMA
        sums = pl.pallas_call(
            functools.partial(kernel, n, detour),
            out_shape=jax.ShapeDtypeStruct((answers, length), jnp.float32),
            in_specs=[
                pl.BlockSpec(memory_space=pl.ANY),
                pl.BlockSpec(memory_space=pltpu.SMEM),
            ],
            out_specs=pl.BlockSpec(memory_space=pltpu.VMEM),
            scratch_shapes=[
                pltpu.VMEM((2, answers, length, width), jnp.bfloat16),
                pltpu.VMEM((4, length, width), jnp.bfloat16),
                pltpu.VMEM((4, length, width), jnp.bfloat16),
                pltpu.VMEM((2, chunks, PIECE, width), jnp.bfloat16),
                pltpu.VMEM((2, ROWS, width), jnp.bfloat16),
                pltpu.VMEM((ROWS, length), jnp.float32),
                pltpu.VMEM((ROWS, length), jnp.float32),
                pltpu.VMEM((4, answers, 128), jnp.int32),
                pltpu.VMEM((4, 1, length), jnp.float32),
                pltpu.VMEM((9, 1, length), jnp.float32),
                pltpu.VMEM((9, 1, length), jnp.float32),
                pltpu.VMEM((8, 1, length), jnp.float32),
                pltpu.VMEM((6, 1, length), jnp.float32),
                dma, dma((2,)), dma((4,)), dma((4,)),
                dma((2, chunks)), dma((4, chunks)), dma((2, chunks)), dma((2, chunks)),
                dma((2, chunks)), dma((2, chunks)), dma((8,)), dma((6,)),
                pltpu.SemaphoreType.REGULAR, pltpu.SemaphoreType.REGULAR,
            ],
            compiler_params=pltpu.CompilerParams(collective_id=0, has_side_effects=True),
            name="consensus",
        )(embeddings, lengths)
        return sums * (math.log(2.0) / (256.0 * (answers - 1 + 4 * answers)))

    return jax.shard_map(
        shards,
        mesh=mesh,
        in_specs=(P(("group", "cand"), None, None), P(("group", "cand"))),
        out_specs=P(("group", "cand"), None),
        check_vma=False,
    )
```

```python
import functools
import math

import jax
import jax.numpy as jnp
from jax import lax
from jax.experimental import pallas as pl
from jax.experimental.pallas import tpu as pltpu
from jax.sharding import PartitionSpec as P

MESH = pl.DeviceIdType.MESH
SCALE = 256.0 * math.log2(math.e)
LOW = -1e30
PIECE = 128
ROWS = 256
WIDE = 256
DETOUR = (3, 2)
PACE = (0, 2, 2, 1, 0, 0, 0, 0)
TURN = 1


def unit_rows(raw):
    values = raw.astype(jnp.float32)
    scale = lax.rsqrt(jnp.sum(values * values, axis=-1, keepdims=True) + 1e-06)
    return (values * scale).astype(jnp.bfloat16)


def kernel(
    n, detour, x_hbm, lens_ref, out_ref,
    raw, units, far, relay, fresh, board_a, board_b, lens, bias, peak, mass, total, back,
    local_sem, near_sems, lens_send, lens_recv, send_sem, far_recv, pass_send, turn_send, relay_recv, relay_send,
    back_send, back_recv, up_sem, down_sem,
):
    length = x_hbm.shape[1]
    chunks = length // PIECE
    per = ROWS // PIECE
    boards = (board_a, board_b)
    group = lax.axis_index("group")
    place = lax.axis_index("cand")
    twin = group + 1 - 2 * lax.rem(group, 2)
    flip = lax.rem(group, 2)
    me = place + flip * (n - 1 - 2 * place)
    role = lax.rem(me, 4)
    core = lax.rem(me, 2)
    partner = me + 1 - 2 * core
    even, odd = role < 2, role >= 2

    def spot(m):
        m = lax.rem(m + n, n)
        return m + flip * (n - 1 - 2 * m)

    def ring(m):
        return (group, spot(m))

    across = (twin, place)
    corner = (twin, spot(jnp.where(even, me + 2, me - 2)))

    for a in range(2):
        lens[0, a : a + 1] = jnp.full((1, 128), lens_ref[a], jnp.int32)

    barrier = pltpu.get_barrier_semaphore()
    quad, quads = me // 4, n // 4
    below, above = quad > 0, quad < quads - 1
    meets = [ring(me - role + lax.rem(role + i, 4)) for i in range(1, 4)] + [across, corner]
    for device in meets:
        pl.semaphore_signal(barrier, inc=1, device_id=device, device_id_type=MESH)

    @pl.when(below)
    def _():
        pl.semaphore_signal(barrier, inc=1, device_id=ring(me - 4), device_id_type=MESH)

    @pl.when(above)
    def _():
        pl.semaphore_signal(barrier, inc=1, device_id=ring(me + 4), device_id_type=MESH)

    local = pltpu.make_async_copy(x_hbm, raw.at[0], local_sem)
    local.start()
    pl.semaphore_wait(barrier, len(meets) + below.astype(jnp.int32) + above.astype(jnp.int32))

    def rise():
        @pl.when(below)
        def _():
            pl.semaphore_wait(up_sem, 1)

        @pl.when(above)
        def _():
            pl.semaphore_signal(up_sem, inc=1, device_id=ring(me + 4), device_id_type=MESH)

    def fall():
        @pl.when(above)
        def _():
            pl.semaphore_wait(down_sem, 1)

        @pl.when(below)
        def _():
            pl.semaphore_signal(down_sem, inc=1, device_id=ring(me - 4), device_id_type=MESH)

    def remote(src, dst, send, recv, device):
        return pltpu.make_async_remote_copy(
            src_ref=src, dst_ref=dst, send_sem=send, recv_sem=recv,
            device_id=device, device_id_type=MESH,
        )

    def rows_of(k):
        return pl.ds(pl.multiple_of(k * PIECE, PIECE), PIECE)

    def spread(i, slot, device):
        return remote(lens.at[0], lens.at[slot], lens_send.at[i], lens_recv.at[slot], device)

    def further():
        target = jnp.where(even, me + 4, me - 4)
        return remote(lens.at[2], lens.at[3], lens_send.at[3], lens_recv.at[3], ring(target))

    def meet_far():
        @pl.when(2 * quad < quads)
        def _():
            rise()
            fall()

        @pl.when(2 * quad >= quads)
        def _():
            fall()
            rise()

    near = remote(x_hbm, raw.at[1], near_sems.at[0], near_sems.at[1], ring(partner))

    def piece(src, a, k, slot, device):
        return remote(src.at[a, rows_of(k)], far.at[slot, rows_of(k)], send_sem.at[a, k], far_recv.at[slot, k], device)

    def around(a, k):
        return remote(x_hbm.at[a, rows_of(k)], relay.at[a, k], turn_send.at[a, k], relay_recv.at[a, k], corner)

    def bypass(a, k):
        return remote(relay.at[a, k], far.at[a, rows_of(k)], relay_send.at[a, k], far_recv.at[a, k], across)

    routed = [(a, k) for k in range(chunks) for a in range(2) if k < detour[a]]
    starts = [min(sum(PACE[:i]), len(routed)) for i in range(len(PACE))] + [len(routed)]
    direct = [[k for k in range(chunks) if (a, k) not in routed] for a in range(2)]

    spread(0, 1, ring(partner)).start()

    @pl.when(odd)
    def _():
        spread(1, 2, ring(me - 2)).start()

    @pl.when(role == 0)
    def _():
        spread(1, 2, ring(me + 2)).start()
        spread(2, 2, ring(me + 3)).start()

    @pl.when(role != 0)
    def _():
        near.start()

    @pl.when(role == 0)
    def _():
        for k in range(chunks):
            for a in range(2):
                piece(x_hbm, a, k, 0, ring(me + 2 + a)).start()

    @pl.when(role == 3)
    def _():
        for k in range(chunks):
            piece(x_hbm, 0, k, 0, ring(me - 2)).start()

    @pl.when(odd)
    def _():
        near.wait_recv()

    @pl.when(role == 2)
    def _():
        for k in range(chunks):
            piece(raw.at[1], 1, k, 1, ring(me - 1)).start()
        for k in direct[0]:
            piece(x_hbm, 0, k, 0, ring(me - 2)).start()

    @pl.when(role == 3)
    def _():
        for k in direct[1]:
            piece(raw.at[1], 1, k, 1, ring(me - 3)).start()

    meet_far()
    lane = lax.broadcasted_iota(jnp.int32, (1, length), 1)
    row = lax.broadcasted_iota(jnp.int32, (PIECE, 128), 0)
    eye = lax.broadcasted_iota(jnp.int32, (PIECE, PIECE), 0) == lax.broadcasted_iota(
        jnp.int32, (PIECE, PIECE), 1
    )
    total[...] = jnp.zeros_like(total)
    peak[...] = jnp.full_like(peak, LOW)
    mass[...] = jnp.zeros_like(mass)

    def set_bias(slot, counts):
        for a in range(2):
            bias[slot + a] = jnp.where(lane < counts[a : a + 1, 0:1], 0.0, LOW)

    def normalise(slot):
        def one(i, carry):
            a, k = i // chunks, lax.rem(i, chunks)
            units[2 * slot + a, rows_of(k)] = unit_rows(raw[slot, a, rows_of(k)])
            return carry

        lax.fori_loop(0, 2 * chunks, one, 0)

    def unit(query, left, count, halves):
        for a in range(count):
            for j in range(0, length, WIDE):
                boards[a][:, j : j + WIDE] = lax.dot_general(
                    query, units[left + a, j : j + WIDE], (((1,), (1,)), ((), ())),
                    preferred_element_type=jnp.float32,
                )
        for h, (counts, first, pair, slot) in enumerate(halves):
            part = slice(h * PIECE, (h + 1) * PIECE)
            row_bias = jnp.where(row + first < counts, 0.0, LOW)
            term = None
            for a in range(count):
                value = soften(boards[a], part, left + a, pair + a, row_bias)
                term = value if term is None else term + value
            cols = pl.ds(pl.multiple_of(first, PIECE), PIECE)
            total[slot, :, cols] = total[slot, :, cols] + jnp.sum(
                jnp.where(eye, jnp.broadcast_to(term, (PIECE, PIECE)), 0.0), axis=0, keepdims=True
            )

    def soften(board, part, left, pair, row_bias):
        tops = None
        for j in range(0, length, 128):
            cols = slice(j, j + 128)
            scores = board[part, cols] * SCALE + bias[left, :, cols] + row_bias
            board[part, cols] = scores
            tops = scores if tops is None else jnp.maximum(tops, scores)
            before = peak[pair, :, cols]
            now = jnp.maximum(before, jnp.max(scores, axis=0, keepdims=True))
            peak[pair, :, cols] = now
            mass[pair, :, cols] = mass[pair, :, cols] * jnp.exp2(before - now)
        top = jnp.max(tops, axis=1, keepdims=True)
        wide = jnp.broadcast_to(top, (PIECE, 128))
        sums = None
        for j in range(0, length, 128):
            cols = slice(j, j + 128)
            scores = board[part, cols]
            value = jnp.exp2(scores - wide)
            sums = value if sums is None else sums + value
            value = jnp.exp2(scores - peak[pair, :, cols])
            mass[pair, :, cols] = mass[pair, :, cols] + jnp.sum(value, axis=0, keepdims=True)
        return top + jnp.log2(jnp.sum(sums, axis=1, keepdims=True))

    def close(slot, pair):
        total[slot] = total[slot] + peak[pair] + jnp.log2(mass[pair])

    local.wait()
    set_bias(0, lens[0])
    normalise(0)
    spread(0, 1, ring(partner)).wait_recv()
    spread(1, 2, ring(partner)).wait_recv()

    @pl.when(role != 0)
    def _():
        further().start()

    @pl.when(role == 0)
    def _():
        near.wait_recv()

    @pl.when(role != 1)
    def _():
        set_bias(2, lens[1])
        normalise(1)

    base = jnp.where((role == 0) | (role == 3), 2, 0)
    last = jnp.where(role >= 2, 2 - base, base)

    def arrive(slot, k):
        remote(x_hbm.at[0, rows_of(k)], far.at[slot, rows_of(k)], pass_send.at[0, 0], far_recv.at[slot, k], across).wait_recv()

    def passing(slot, k):
        target = jnp.where(even, me + 4, me - 4)
        there = jnp.where(even, slot + 2, slot + 1)
        return remote(far.at[slot, rows_of(k)], far.at[there, rows_of(k)], pass_send.at[slot, k], far_recv.at[there, k], ring(target))

    def hand_on(slot, k):
        arrive(slot, k)
        passing(slot, k).start()

    def tile_rows(tile):
        return pl.ds(pl.multiple_of(tile * ROWS, ROWS), ROWS)

    def take_local(slot, k, stage, h):
        fresh[stage, h * PIECE : (h + 1) * PIECE] = units[slot, rows_of(k)]

    def take_far(slot, k, stage, h):
        fresh[stage, h * PIECE : (h + 1) * PIECE] = unit_rows(far[slot, rows_of(k)])

    own_len = [lens[0, a : a + 1] for a in range(2)]
    is0, is1, is2, is3 = (jnp.full((1, 128), role, jnp.int32) == r for r in range(4))
    pick = lambda v0, v1, v2, v3: jnp.where(is0, v0, jnp.where(is1, v1, jnp.where(is2, v2, v3)))

    def lens_at(slot, a):
        return lens[slot, a : a + 1]

    def soon():
        return (
            pick(own_len[0], lens_at(2, 0), lens_at(1, 0), own_len[1]),
            pick(own_len[1], lens_at(2, 1), lens_at(2, 0), lens_at(2, 1)),
        )

    def later():
        return (
            pick(lens_at(2, 0), lens_at(3, 0), lens_at(3, 0), lens_at(3, 1)),
            pick(lens_at(2, 1), lens_at(3, 1), lens_at(3, 0), lens_at(3, 1)),
        )

    choose = lambda v0, v1, v2, v3: jnp.where(role == 0, v0, jnp.where(role == 1, v1, jnp.where(role == 2, v2, v3)))
    slots = [choose(0, 4, 2, 1), choose(1, 5, 4, 4), choose(4, 6, 5, 5), choose(5, 7, 5, 5)]

    def routes(j, act):
        for i in range(len(PACE)):
            if starts[i] < starts[i + 1]:
                @pl.when(j == i)
                def _():
                    for a, k in routed[starts[i] : starts[i + 1]]:
                        act(a, k)

    def turn(a, k):
        around(a, k).wait_recv()
        bypass(a, k).start()

    lag = jnp.where(role == 0, chunks, per)

    def step(j, carry):
        @pl.when(role == 2)
        def _():
            routes(j, lambda a, k: around(a, k).start())

        @pl.when(j < chunks)
        def _():
            @pl.when(role == 1)
            def _():
                hand_on(0, j)
                take_far(0, j, 0, 0)

            @pl.when(role != 1)
            def _():
                take_local(choose(0, 0, 2, 1), j, 0, 0)

            @pl.when(role == 0)
            def _():
                take_local(1, j, 0, 1)

            @pl.when(role != 0)
            def _():
                slot = jnp.where(role == 1, 1, 0)
                hand_on(slot, j)
                take_far(slot, j, 0, 1)

            counts = soon()
            unit(fresh[0], base, 2, [(counts[0], j * PIECE, 0, slots[0]), (counts[1], j * PIECE, 2, slots[1])])

            @pl.when(lax.rem(j, per) == 0)
            def _():
                unit(units[1, tile_rows(j // per)], 0, 1, [(own_len[1], (j + h) * PIECE, 8, 1) for h in range(per)])

        @pl.when((j >= lag) & (j < lag + chunks))
        def _():
            k = j - lag
            late = lax.rem(k, per)

            @pl.when((j == lag) & (role != 0))
            def _():
                further().wait_recv()


            @pl.when(even)
            def _():
                for h in range(2):
                    slot = choose(h, 2 + h, 0, 0)
                    arrive(slot, k)
                    take_far(slot, k, 1, h)

            @pl.when(odd & (late == 0))
            def _():
                for h in range(per):
                    arrive(1, k + h)
                    take_far(1, k + h, 1, h)

            left = jnp.where(late == 0, base, last)
            counts = later()
            unit(
                fresh[1], left, 2,
                [
                    (counts[0], jnp.where(even, k, k - late) * PIECE, jnp.where(even, 4, 4 + 2 * late), slots[2]),
                    (counts[1], jnp.where(even, k, k - late + 1) * PIECE, jnp.where(even, 6, 4 + 2 * late), slots[3]),
                ],
            )

        @pl.when(role == 3)
        def _():
            routes(j - TURN, turn)

        return carry

    lax.fori_loop(0, lag + chunks, step, 0)

    def give(src, dst, device):
        return remote(total.at[src], back.at[dst], back_send.at[src], back_recv.at[dst], device)

    gives = (
        [give(4, 2, ring(me + 2)), give(5, 3, ring(me + 2))],
        [give(6, 4, ring(me - 2)), give(7, 5, ring(me - 2)), give(4, 2, ring(me + 2)), give(5, 3, ring(me + 2))],
        [give(5, 4, ring(me + 2)), give(4, 2, ring(me - 2))],
        [give(5, 5, ring(me + 1)), give(4, 3, ring(me - 3))],
    )
    for r in range(4):
        @pl.when(role == r)
        def _():
            for copy in gives[r]:
                copy.start()

    close(0, 8)
    for s in range(4):
        left = last if s == 3 else base
        for a in range(2):
            close(left + a, 2 * s + a)

    @pl.when(role != 1)
    def _():
        for a in range(2):
            give(2 + a, a, ring(partner)).start()

    takes = ([2, 3, 4, 5], [0, 1], [0, 1, 2, 3], [0, 1, 2, 3, 4, 5])
    for r in range(4):
        @pl.when(role == r)
        def _():
            for b in takes[r]:
                give(0, b, ring(partner)).wait_recv()
            for a in range(2):
                whole = total[a]
                for b in takes[r]:
                    if b % 2 == a:
                        whole = whole + back[b]
                out_ref[a : a + 1] = jnp.where(bias[a] == 0.0, whole, 0.0)
            for copy in gives[r]:
                copy.wait_send()

    @pl.when(role != 1)
    def _():
        for a in range(2):
            give(2 + a, a, ring(partner)).wait_send()

    spread(0, 1, ring(partner)).wait_send()

    @pl.when(role != 1)
    def _():
        spread(1, 2, ring(partner)).wait_send()

    @pl.when(role == 0)
    def _():
        spread(2, 2, ring(partner)).wait_send()

    @pl.when(role != 0)
    def _():
        further().wait_send()

    @pl.when(role != 0)
    def _():
        near.wait_send()

    def sent(a, pieces):
        for k in pieces:
            piece(x_hbm, a, k, a, ring(partner)).wait_send()

    @pl.when(role == 0)
    def _():
        sent(0, range(chunks))
        sent(1, range(chunks))

    @pl.when(role == 2)
    def _():
        sent(1, range(chunks))
        sent(0, direct[0])
        for a, k in routed:
            around(a, k).wait_send()

    @pl.when(role == 3)
    def _():
        sent(0, range(chunks))
        sent(1, direct[1])

    @pl.when(role == 1)
    def _():
        for k in range(chunks):
            for a in range(2):
                passing(a, k).wait_send()

    @pl.when(odd)
    def _():
        for k in range(chunks):
            passing(0, k).wait_send()

    @pl.when(role == 3)
    def _():
        for a, k in routed:
            bypass(a, k).wait_send()


def solution(mesh):
    n = mesh.shape["cand"]
    detour = DETOUR if mesh.shape["group"] % 2 == 0 else (0, 0)

    def shards(embeddings, lengths):
        answers, length, width = embeddings.shape
        chunks = length // PIECE
        dma = pltpu.SemaphoreType.DMA
        sums = pl.pallas_call(
            functools.partial(kernel, n, detour),
            out_shape=jax.ShapeDtypeStruct((answers, length), jnp.float32),
            in_specs=[
                pl.BlockSpec(memory_space=pl.ANY),
                pl.BlockSpec(memory_space=pltpu.SMEM),
            ],
            out_specs=pl.BlockSpec(memory_space=pltpu.VMEM),
            scratch_shapes=[
                pltpu.VMEM((2, answers, length, width), jnp.bfloat16),
                pltpu.VMEM((4, length, width), jnp.bfloat16),
                pltpu.VMEM((4, length, width), jnp.bfloat16),
                pltpu.VMEM((2, chunks, PIECE, width), jnp.bfloat16),
                pltpu.VMEM((2, ROWS, width), jnp.bfloat16),
                pltpu.VMEM((ROWS, length), jnp.float32),
                pltpu.VMEM((ROWS, length), jnp.float32),
                pltpu.VMEM((4, answers, 128), jnp.int32),
                pltpu.VMEM((4, 1, length), jnp.float32),
                pltpu.VMEM((9, 1, length), jnp.float32),
                pltpu.VMEM((9, 1, length), jnp.float32),
                pltpu.VMEM((8, 1, length), jnp.float32),
                pltpu.VMEM((6, 1, length), jnp.float32),
                dma, dma((2,)), dma((4,)), dma((4,)),
                dma((2, chunks)), dma((4, chunks)), dma((2, chunks)), dma((2, chunks)),
                dma((2, chunks)), dma((2, chunks)), dma((8,)), dma((6,)),
                pltpu.SemaphoreType.REGULAR, pltpu.SemaphoreType.REGULAR,
            ],
            compiler_params=pltpu.CompilerParams(collective_id=0, has_side_effects=True),
            name="consensus",
        )(embeddings, lengths)
        return sums * (math.log(2.0) / (256.0 * (answers - 1 + 4 * answers)))

    return jax.shard_map(
        shards,
        mesh=mesh,
        in_specs=(P(("group", "cand"), None, None), P(("group", "cand"))),
        out_specs=P(("group", "cand"), None),
        check_vma=False,
    )
```

```python
import functools
import math

import jax
import jax.numpy as jnp
from jax import lax
from jax.experimental import pallas as pl
from jax.experimental.pallas import tpu as pltpu
from jax.sharding import PartitionSpec as P

MESH = pl.DeviceIdType.MESH
SCALE = 256.0 * math.log2(math.e)
LOW = -1e30
PIECE = 128
ROWS = 256
WIDE = 256
DETOUR = (3, 2)
PACE = (0, 2, 2, 1, 0, 0, 0, 0)
TURN = 1


def unit_rows(raw):
    values = raw.astype(jnp.float32)
    scale = lax.rsqrt(jnp.sum(values * values, axis=-1, keepdims=True) + 1e-06)
    return (values * scale).astype(jnp.bfloat16)


def kernel(
    n, detour, x_hbm, lens_ref, out_ref,
    raw, units, far, relay, fresh, board_a, board_b, lens, bias, peak, mass, total, back,
    local_sem, near_sems, lens_send, lens_recv, send_sem, far_recv, pass_send, turn_send, relay_recv, relay_send,
    back_send, back_recv, up_sem, down_sem,
):
    length = x_hbm.shape[1]
    chunks = length // PIECE
    per = ROWS // PIECE
    boards = (board_a, board_b)
    group = lax.axis_index("group")
    place = lax.axis_index("cand")
    twin = group + 1 - 2 * lax.rem(group, 2)
    flip = lax.rem(group, 2)
    me = place + flip * (n - 1 - 2 * place)
    role = lax.rem(me, 4)
    core = lax.rem(me, 2)
    partner = me + 1 - 2 * core
    even, odd = role < 2, role >= 2

    def spot(m):
        m = lax.rem(m + n, n)
        return m + flip * (n - 1 - 2 * m)

    def ring(m):
        return (group, spot(m))

    across = (twin, place)
    corner = (twin, spot(jnp.where(even, me + 2, me - 2)))

    for a in range(2):
        lens[0, a : a + 1] = jnp.full((1, 128), lens_ref[a], jnp.int32)

    barrier = pltpu.get_barrier_semaphore()
    quad, quads = me // 4, n // 4
    below, above = quad > 0, quad < quads - 1
    meets = [ring(me - role + lax.rem(role + i, 4)) for i in range(1, 4)] + [across, corner]
    for device in meets:
        pl.semaphore_signal(barrier, inc=1, device_id=device, device_id_type=MESH)

    @pl.when(below)
    def _():
        pl.semaphore_signal(barrier, inc=1, device_id=ring(me - 4), device_id_type=MESH)

    @pl.when(above)
    def _():
        pl.semaphore_signal(barrier, inc=1, device_id=ring(me + 4), device_id_type=MESH)

    local = pltpu.make_async_copy(x_hbm, raw.at[0], local_sem)
    local.start()
    pl.semaphore_wait(barrier, len(meets) + below.astype(jnp.int32) + above.astype(jnp.int32))

    def rise():
        @pl.when(below)
        def _():
            pl.semaphore_wait(up_sem, 1)

        @pl.when(above)
        def _():
            pl.semaphore_signal(up_sem, inc=1, device_id=ring(me + 4), device_id_type=MESH)

    def fall():
        @pl.when(above)
        def _():
            pl.semaphore_wait(down_sem, 1)

        @pl.when(below)
        def _():
            pl.semaphore_signal(down_sem, inc=1, device_id=ring(me - 4), device_id_type=MESH)

    def remote(src, dst, send, recv, device):
        return pltpu.make_async_remote_copy(
            src_ref=src, dst_ref=dst, send_sem=send, recv_sem=recv,
            device_id=device, device_id_type=MESH,
        )

    def rows_of(k):
        return pl.ds(pl.multiple_of(k * PIECE, PIECE), PIECE)

    def spread(i, slot, device):
        return remote(lens.at[0], lens.at[slot], lens_send.at[i], lens_recv.at[slot], device)

    def further():
        target = jnp.where(even, me + 4, me - 4)
        return remote(lens.at[2], lens.at[3], lens_send.at[3], lens_recv.at[3], ring(target))

    def meet_far():
        @pl.when(2 * quad < quads)
        def _():
            rise()
            fall()

        @pl.when(2 * quad >= quads)
        def _():
            fall()
            rise()

    near = remote(x_hbm, raw.at[1], near_sems.at[0], near_sems.at[1], ring(partner))

    def piece(src, a, k, slot, device):
        return remote(src.at[a, rows_of(k)], far.at[slot, rows_of(k)], send_sem.at[a, k], far_recv.at[slot, k], device)

    def around(a, k):
        return remote(x_hbm.at[a, rows_of(k)], relay.at[a, k], turn_send.at[a, k], relay_recv.at[a, k], corner)

    def bypass(a, k):
        return remote(relay.at[a, k], far.at[a, rows_of(k)], relay_send.at[a, k], far_recv.at[a, k], across)

    routed = [(a, k) for k in range(chunks) for a in range(2) if k < detour[a]]
    starts = [min(sum(PACE[:i]), len(routed)) for i in range(len(PACE))] + [len(routed)]
    direct = [[k for k in range(chunks) if (a, k) not in routed] for a in range(2)]

    spread(0, 1, ring(partner)).start()

    @pl.when(odd)
    def _():
        spread(1, 2, ring(me - 2)).start()

    @pl.when(role == 0)
    def _():
        spread(1, 2, ring(me + 2)).start()
        spread(2, 2, ring(me + 3)).start()

    @pl.when(role != 0)
    def _():
        near.start()

    @pl.when(role == 0)
    def _():
        for k in range(chunks):
            for a in range(2):
                piece(x_hbm, a, k, 0, ring(me + 2 + a)).start()

    @pl.when(role == 3)
    def _():
        for k in range(chunks):
            piece(x_hbm, 0, k, 0, ring(me - 2)).start()

    @pl.when(odd)
    def _():
        near.wait_recv()

    @pl.when(role == 2)
    def _():
        for k in range(chunks):
            piece(raw.at[1], 1, k, 1, ring(me - 1)).start()
        for k in direct[0]:
            piece(x_hbm, 0, k, 0, ring(me - 2)).start()

    @pl.when(role == 3)
    def _():
        for k in direct[1]:
            piece(raw.at[1], 1, k, 1, ring(me - 3)).start()

    meet_far()
    lane = lax.broadcasted_iota(jnp.int32, (1, length), 1)
    row = lax.broadcasted_iota(jnp.int32, (PIECE, 128), 0)
    eye = lax.broadcasted_iota(jnp.int32, (PIECE, PIECE), 0) == lax.broadcasted_iota(
        jnp.int32, (PIECE, PIECE), 1
    )
    total[...] = jnp.zeros_like(total)
    peak[...] = jnp.full_like(peak, LOW)
    mass[...] = jnp.zeros_like(mass)

    def set_bias(slot, counts):
        for a in range(2):
            bias[slot + a] = jnp.where(lane < counts[a : a + 1, 0:1], 0.0, LOW)

    def normalise(slot):
        def one(i, carry):
            a, k = i // chunks, lax.rem(i, chunks)
            units[2 * slot + a, rows_of(k)] = unit_rows(raw[slot, a, rows_of(k)])
            return carry

        lax.fori_loop(0, 2 * chunks, one, 0)

    def unit(query, left, count, halves):
        for a in range(count):
            for j in range(0, length, WIDE):
                boards[a][:, j : j + WIDE] = lax.dot_general(
                    query, units[left + a, j : j + WIDE], (((1,), (1,)), ((), ())),
                    preferred_element_type=jnp.float32,
                )
        for h, (counts, first, pair, slot) in enumerate(halves):
            part = slice(h * PIECE, (h + 1) * PIECE)
            row_bias = jnp.where(row + first < counts, 0.0, LOW)
            term = None
            for a in range(count):
                value = soften(boards[a], part, left + a, pair + a, row_bias)
                term = value if term is None else term + value
            cols = pl.ds(pl.multiple_of(first, PIECE), PIECE)
            total[slot, :, cols] = total[slot, :, cols] + jnp.sum(
                jnp.where(eye, jnp.broadcast_to(term, (PIECE, PIECE)), 0.0), axis=0, keepdims=True
            )

    def soften(board, part, left, pair, row_bias):
        tops = None
        for j in range(0, length, 128):
            cols = slice(j, j + 128)
            scores = board[part, cols] * SCALE + bias[left, :, cols] + row_bias
            board[part, cols] = scores
            tops = scores if tops is None else jnp.maximum(tops, scores)
            before = peak[pair, :, cols]
            now = jnp.maximum(before, jnp.max(scores, axis=0, keepdims=True))
            peak[pair, :, cols] = now
            mass[pair, :, cols] = mass[pair, :, cols] * jnp.exp2(before - now)
        top = jnp.max(tops, axis=1, keepdims=True)
        wide = jnp.broadcast_to(top, (PIECE, 128))
        sums = None
        for j in range(0, length, 128):
            cols = slice(j, j + 128)
            scores = board[part, cols]
            value = jnp.exp2(scores - wide)
            sums = value if sums is None else sums + value
            value = jnp.exp2(scores - peak[pair, :, cols])
            mass[pair, :, cols] = mass[pair, :, cols] + jnp.sum(value, axis=0, keepdims=True)
        return top + jnp.log2(jnp.sum(sums, axis=1, keepdims=True))

    def close(slot, pair):
        total[slot] = total[slot] + peak[pair] + jnp.log2(mass[pair])

    local.wait()
    set_bias(0, lens[0])
    normalise(0)
    spread(0, 1, ring(partner)).wait_recv()
    spread(1, 2, ring(partner)).wait_recv()

    @pl.when(role != 0)
    def _():
        further().start()

    @pl.when(role == 0)
    def _():
        near.wait_recv()

    @pl.when(role != 1)
    def _():
        set_bias(2, lens[1])
        normalise(1)

    base = jnp.where((role == 0) | (role == 3), 2, 0)
    last = jnp.where(role >= 2, 2 - base, base)

    def arrive(slot, k):
        remote(x_hbm.at[0, rows_of(k)], far.at[slot, rows_of(k)], pass_send.at[0, 0], far_recv.at[slot, k], across).wait_recv()

    def passing(slot, k):
        target = jnp.where(even, me + 4, me - 4)
        there = jnp.where(even, slot + 2, slot + 1)
        return remote(far.at[slot, rows_of(k)], far.at[there, rows_of(k)], pass_send.at[slot, k], far_recv.at[there, k], ring(target))

    def hand_on(slot, k):
        arrive(slot, k)
        passing(slot, k).start()

    def tile_rows(tile):
        return pl.ds(pl.multiple_of(tile * ROWS, ROWS), ROWS)

    def take_local(slot, k, stage, h):
        fresh[stage, h * PIECE : (h + 1) * PIECE] = units[slot, rows_of(k)]

    def take_far(slot, k, stage, h):
        fresh[stage, h * PIECE : (h + 1) * PIECE] = unit_rows(far[slot, rows_of(k)])

    own_len = [lens[0, a : a + 1] for a in range(2)]
    is0, is1, is2, is3 = (jnp.full((1, 128), role, jnp.int32) == r for r in range(4))
    pick = lambda v0, v1, v2, v3: jnp.where(is0, v0, jnp.where(is1, v1, jnp.where(is2, v2, v3)))

    def lens_at(slot, a):
        return lens[slot, a : a + 1]

    def soon():
        return (
            pick(own_len[0], lens_at(2, 0), lens_at(1, 0), own_len[1]),
            pick(own_len[1], lens_at(2, 1), lens_at(2, 0), lens_at(2, 1)),
        )

    def later():
        return (
            pick(lens_at(2, 0), lens_at(3, 0), lens_at(3, 0), lens_at(3, 1)),
            pick(lens_at(2, 1), lens_at(3, 1), lens_at(3, 0), lens_at(3, 1)),
        )

    choose = lambda v0, v1, v2, v3: jnp.where(role == 0, v0, jnp.where(role == 1, v1, jnp.where(role == 2, v2, v3)))
    slots = [choose(0, 4, 2, 1), choose(1, 5, 4, 4), choose(4, 6, 5, 5), choose(5, 7, 5, 5)]

    def routes(j, act):
        for i in range(len(PACE)):
            if starts[i] < starts[i + 1]:
                @pl.when(j == i)
                def _():
                    for a, k in routed[starts[i] : starts[i + 1]]:
                        act(a, k)

    def turn(a, k):
        around(a, k).wait_recv()
        bypass(a, k).start()

    lag = jnp.where(role == 0, chunks, per)

    def step(j, carry):
        @pl.when(j == chunks)
        def _():
            close(0, 8)
            for s in range(2):
                for a in range(2):
                    close(base + a, 2 * s + a)

        @pl.when(role == 2)
        def _():
            routes(j, lambda a, k: around(a, k).start())

        @pl.when(j < chunks)
        def _():
            @pl.when(role == 1)
            def _():
                hand_on(0, j)
                take_far(0, j, 0, 0)

            @pl.when(role != 1)
            def _():
                take_local(choose(0, 0, 2, 1), j, 0, 0)

            @pl.when(role == 0)
            def _():
                take_local(1, j, 0, 1)

            @pl.when(role != 0)
            def _():
                slot = jnp.where(role == 1, 1, 0)
                hand_on(slot, j)
                take_far(slot, j, 0, 1)

            counts = soon()
            unit(fresh[0], base, 2, [(counts[0], j * PIECE, 0, slots[0]), (counts[1], j * PIECE, 2, slots[1])])

            @pl.when(lax.rem(j, per) == 0)
            def _():
                unit(units[1, tile_rows(j // per)], 0, 1, [(own_len[1], (j + h) * PIECE, 8, 1) for h in range(per)])

        @pl.when((j >= lag) & (j < lag + chunks))
        def _():
            k = j - lag
            late = lax.rem(k, per)

            @pl.when((j == lag) & (role != 0))
            def _():
                further().wait_recv()


            @pl.when(even)
            def _():
                for h in range(2):
                    slot = choose(h, 2 + h, 0, 0)
                    arrive(slot, k)
                    take_far(slot, k, 1, h)

            @pl.when(odd & (late == 0))
            def _():
                for h in range(per):
                    arrive(1, k + h)
                    take_far(1, k + h, 1, h)

            left = jnp.where(late == 0, base, last)
            counts = later()
            unit(
                fresh[1], left, 2,
                [
                    (counts[0], jnp.where(even, k, k - late) * PIECE, jnp.where(even, 4, 4 + 2 * late), slots[2]),
                    (counts[1], jnp.where(even, k, k - late + 1) * PIECE, jnp.where(even, 6, 4 + 2 * late), slots[3]),
                ],
            )

        @pl.when(role == 3)
        def _():
            routes(j - TURN, turn)

        return carry

    lax.fori_loop(0, lag + chunks, step, 0)

    def give(src, dst, device):
        return remote(total.at[src], back.at[dst], back_send.at[src], back_recv.at[dst], device)

    gives = (
        [give(4, 2, ring(me + 2)), give(5, 3, ring(me + 2))],
        [give(6, 4, ring(me - 2)), give(7, 5, ring(me - 2)), give(4, 2, ring(me + 2)), give(5, 3, ring(me + 2))],
        [give(5, 4, ring(me + 2)), give(4, 2, ring(me - 2))],
        [give(5, 5, ring(me + 1)), give(4, 3, ring(me - 3))],
    )
    for r in range(4):
        @pl.when(role == r)
        def _():
            for copy in gives[r]:
                copy.start()

    for s in range(2, 4):
        left = last if s == 3 else base
        for a in range(2):
            close(left + a, 2 * s + a)

    @pl.when(role != 1)
    def _():
        for a in range(2):
            give(2 + a, a, ring(partner)).start()

    takes = ([2, 3, 4, 5], [0, 1], [0, 1, 2, 3], [0, 1, 2, 3, 4, 5])
    for r in range(4):
        @pl.when(role == r)
        def _():
            for b in takes[r]:
                give(0, b, ring(partner)).wait_recv()
            for a in range(2):
                whole = total[a]
                for b in takes[r]:
                    if b % 2 == a:
                        whole = whole + back[b]
                out_ref[a : a + 1] = jnp.where(bias[a] == 0.0, whole, 0.0)
            for copy in gives[r]:
                copy.wait_send()

    @pl.when(role != 1)
    def _():
        for a in range(2):
            give(2 + a, a, ring(partner)).wait_send()

    spread(0, 1, ring(partner)).wait_send()

    @pl.when(role != 1)
    def _():
        spread(1, 2, ring(partner)).wait_send()

    @pl.when(role == 0)
    def _():
        spread(2, 2, ring(partner)).wait_send()

    @pl.when(role != 0)
    def _():
        further().wait_send()

    @pl.when(role != 0)
    def _():
        near.wait_send()

    def sent(a, pieces):
        for k in pieces:
            piece(x_hbm, a, k, a, ring(partner)).wait_send()

    @pl.when(role == 0)
    def _():
        sent(0, range(chunks))
        sent(1, range(chunks))

    @pl.when(role == 2)
    def _():
        sent(1, range(chunks))
        sent(0, direct[0])
        for a, k in routed:
            around(a, k).wait_send()

    @pl.when(role == 3)
    def _():
        sent(0, range(chunks))
        sent(1, direct[1])

    @pl.when(role == 1)
    def _():
        for k in range(chunks):
            for a in range(2):
                passing(a, k).wait_send()

    @pl.when(odd)
    def _():
        for k in range(chunks):
            passing(0, k).wait_send()

    @pl.when(role == 3)
    def _():
        for a, k in routed:
            bypass(a, k).wait_send()


def solution(mesh):
    n = mesh.shape["cand"]
    detour = DETOUR if mesh.shape["group"] % 2 == 0 else (0, 0)

    def shards(embeddings, lengths):
        answers, length, width = embeddings.shape
        chunks = length // PIECE
        dma = pltpu.SemaphoreType.DMA
        sums = pl.pallas_call(
            functools.partial(kernel, n, detour),
            out_shape=jax.ShapeDtypeStruct((answers, length), jnp.float32),
            in_specs=[
                pl.BlockSpec(memory_space=pl.ANY),
                pl.BlockSpec(memory_space=pltpu.SMEM),
            ],
            out_specs=pl.BlockSpec(memory_space=pltpu.VMEM),
            scratch_shapes=[
                pltpu.VMEM((2, answers, length, width), jnp.bfloat16),
                pltpu.VMEM((4, length, width), jnp.bfloat16),
                pltpu.VMEM((4, length, width), jnp.bfloat16),
                pltpu.VMEM((2, chunks, PIECE, width), jnp.bfloat16),
                pltpu.VMEM((2, ROWS, width), jnp.bfloat16),
                pltpu.VMEM((ROWS, length), jnp.float32),
                pltpu.VMEM((ROWS, length), jnp.float32),
                pltpu.VMEM((4, answers, 128), jnp.int32),
                pltpu.VMEM((4, 1, length), jnp.float32),
                pltpu.VMEM((9, 1, length), jnp.float32),
                pltpu.VMEM((9, 1, length), jnp.float32),
                pltpu.VMEM((8, 1, length), jnp.float32),
                pltpu.VMEM((6, 1, length), jnp.float32),
                dma, dma((2,)), dma((4,)), dma((4,)),
                dma((2, chunks)), dma((4, chunks)), dma((2, chunks)), dma((2, chunks)),
                dma((2, chunks)), dma((2, chunks)), dma((8,)), dma((6,)),
                pltpu.SemaphoreType.REGULAR, pltpu.SemaphoreType.REGULAR,
            ],
            compiler_params=pltpu.CompilerParams(collective_id=0, has_side_effects=True),
            name="consensus",
        )(embeddings, lengths)
        return sums * (math.log(2.0) / (256.0 * (answers - 1 + 4 * answers)))

    return jax.shard_map(
        shards,
        mesh=mesh,
        in_specs=(P(("group", "cand"), None, None), P(("group", "cand"))),
        out_specs=P(("group", "cand"), None),
        check_vma=False,
    )
```

```python
import functools
import math

import jax
import jax.numpy as jnp
from jax import lax
from jax.experimental import pallas as pl
from jax.experimental.pallas import tpu as pltpu
from jax.sharding import PartitionSpec as P

MESH = pl.DeviceIdType.MESH
SCALE = 256.0 * math.log2(math.e)
LOW = -1e30
PIECE = 128
ROWS = 256
WIDE = 256
DETOUR = (3, 2)
PACE = (0, 2, 2, 1, 0, 0, 0, 0)
TURN = 1


def unit_rows(raw):
    values = raw.astype(jnp.float32)
    scale = lax.rsqrt(jnp.sum(values * values, axis=-1, keepdims=True) + 1e-06)
    return (values * scale).astype(jnp.bfloat16)


def kernel(
    n, detour, x_hbm, lens_ref, out_ref,
    raw, units, far, relay, fresh, board_a, board_b, lens, bias, peak, mass, total, back,
    local_sem, near_sems, lens_send, lens_recv, send_sem, far_recv, pass_send, turn_send, relay_recv, relay_send,
    back_send, back_recv, up_sem, down_sem,
):
    length = x_hbm.shape[1]
    chunks = length // PIECE
    per = ROWS // PIECE
    boards = (board_a, board_b)
    group = lax.axis_index("group")
    place = lax.axis_index("cand")
    twin = group + 1 - 2 * lax.rem(group, 2)
    flip = lax.rem(group, 2)
    me = place + flip * (n - 1 - 2 * place)
    role = lax.rem(me, 4)
    core = lax.rem(me, 2)
    partner = me + 1 - 2 * core
    even, odd = role < 2, role >= 2

    def spot(m):
        m = lax.rem(m + n, n)
        return m + flip * (n - 1 - 2 * m)

    def ring(m):
        return (group, spot(m))

    across = (twin, place)
    corner = (twin, spot(jnp.where(even, me + 2, me - 2)))

    for a in range(2):
        lens[0, a : a + 1] = jnp.full((1, 128), lens_ref[a], jnp.int32)

    barrier = pltpu.get_barrier_semaphore()
    quad, quads = me // 4, n // 4
    below, above = quad > 0, quad < quads - 1
    meets = [ring(me - role + lax.rem(role + i, 4)) for i in range(1, 4)] + [across, corner]
    for device in meets:
        pl.semaphore_signal(barrier, inc=1, device_id=device, device_id_type=MESH)

    @pl.when(below)
    def _():
        pl.semaphore_signal(barrier, inc=1, device_id=ring(me - 4), device_id_type=MESH)

    @pl.when(above)
    def _():
        pl.semaphore_signal(barrier, inc=1, device_id=ring(me + 4), device_id_type=MESH)

    local = pltpu.make_async_copy(x_hbm, raw.at[0], local_sem)
    local.start()
    pl.semaphore_wait(barrier, len(meets) + below.astype(jnp.int32) + above.astype(jnp.int32))

    def rise():
        @pl.when(below)
        def _():
            pl.semaphore_wait(up_sem, 1)

        @pl.when(above)
        def _():
            pl.semaphore_signal(up_sem, inc=1, device_id=ring(me + 4), device_id_type=MESH)

    def fall():
        @pl.when(above)
        def _():
            pl.semaphore_wait(down_sem, 1)

        @pl.when(below)
        def _():
            pl.semaphore_signal(down_sem, inc=1, device_id=ring(me - 4), device_id_type=MESH)

    def remote(src, dst, send, recv, device):
        return pltpu.make_async_remote_copy(
            src_ref=src, dst_ref=dst, send_sem=send, recv_sem=recv,
            device_id=device, device_id_type=MESH,
        )

    def rows_of(k):
        return pl.ds(pl.multiple_of(k * PIECE, PIECE), PIECE)

    def spread(i, slot, device):
        return remote(lens.at[0], lens.at[slot], lens_send.at[i], lens_recv.at[slot], device)

    def further():
        target = jnp.where(even, me + 4, me - 4)
        return remote(lens.at[2], lens.at[3], lens_send.at[3], lens_recv.at[3], ring(target))

    def meet_far():
        @pl.when(2 * quad < quads)
        def _():
            rise()
            fall()

        @pl.when(2 * quad >= quads)
        def _():
            fall()
            rise()

    near = remote(x_hbm, raw.at[1], near_sems.at[0], near_sems.at[1], ring(partner))

    def piece(src, a, k, slot, device):
        return remote(src.at[a, rows_of(k)], far.at[slot, rows_of(k)], send_sem.at[a, k], far_recv.at[slot, k], device)

    def around(a, k):
        return remote(x_hbm.at[a, rows_of(k)], relay.at[a, k], turn_send.at[a, k], relay_recv.at[a, k], corner)

    def bypass(a, k):
        return remote(relay.at[a, k], far.at[a, rows_of(k)], relay_send.at[a, k], far_recv.at[a, k], across)

    routed = [(a, k) for k in range(chunks) for a in range(2) if k < detour[a]]
    starts = [min(sum(PACE[:i]), len(routed)) for i in range(len(PACE))] + [len(routed)]
    direct = [[k for k in range(chunks) if (a, k) not in routed] for a in range(2)]

    spread(0, 1, ring(partner)).start()

    @pl.when(odd)
    def _():
        spread(1, 2, ring(me - 2)).start()

    @pl.when(role == 0)
    def _():
        spread(1, 2, ring(me + 2)).start()
        spread(2, 2, ring(me + 3)).start()

    @pl.when(role != 0)
    def _():
        near.start()

    @pl.when(role == 0)
    def _():
        for k in range(chunks):
            for a in range(2):
                piece(x_hbm, a, k, 0, ring(me + 2 + a)).start()

    @pl.when(role == 3)
    def _():
        for k in range(chunks):
            piece(x_hbm, 0, k, 0, ring(me - 2)).start()

    @pl.when(odd)
    def _():
        near.wait_recv()

    @pl.when(role == 2)
    def _():
        for k in range(chunks):
            piece(raw.at[1], 1, k, 1, ring(me - 1)).start()
        for k in direct[0]:
            piece(x_hbm, 0, k, 0, ring(me - 2)).start()

    @pl.when(role == 3)
    def _():
        for k in direct[1]:
            piece(raw.at[1], 1, k, 1, ring(me - 3)).start()

    meet_far()
    lane = lax.broadcasted_iota(jnp.int32, (1, length), 1)
    row = lax.broadcasted_iota(jnp.int32, (PIECE, 128), 0)
    eye = lax.broadcasted_iota(jnp.int32, (PIECE, PIECE), 0) == lax.broadcasted_iota(
        jnp.int32, (PIECE, PIECE), 1
    )
    total[...] = jnp.zeros_like(total)
    peak[...] = jnp.full_like(peak, LOW)
    mass[...] = jnp.zeros_like(mass)

    def set_bias(slot, counts):
        for a in range(2):
            bias[slot + a] = jnp.where(lane < counts[a : a + 1, 0:1], 0.0, LOW)

    def normalise(slot):
        def one(i, carry):
            a, k = i // chunks, lax.rem(i, chunks)
            units[2 * slot + a, rows_of(k)] = unit_rows(raw[slot, a, rows_of(k)])
            return carry

        lax.fori_loop(0, 2 * chunks, one, 0)

    def unit(query, left, count, halves):
        for a in range(count):
            for j in range(0, length, WIDE):
                boards[a][:, j : j + WIDE] = lax.dot_general(
                    query, units[left + a, j : j + WIDE], (((1,), (1,)), ((), ())),
                    preferred_element_type=jnp.float32,
                )
        for h, (counts, first, pair, slot) in enumerate(halves):
            part = slice(h * PIECE, (h + 1) * PIECE)
            row_bias = jnp.where(row + first < counts, 0.0, LOW)
            term = None
            for a in range(count):
                value = soften(boards[a], part, left + a, pair + a, row_bias)
                term = value if term is None else term + value
            cols = pl.ds(pl.multiple_of(first, PIECE), PIECE)
            total[slot, :, cols] = total[slot, :, cols] + jnp.sum(
                jnp.where(eye, jnp.broadcast_to(term, (PIECE, PIECE)), 0.0), axis=0, keepdims=True
            )

    def soften(board, part, left, pair, row_bias):
        tops = None
        for j in range(0, length, 128):
            cols = slice(j, j + 128)
            scores = board[part, cols] * SCALE + bias[left, :, cols] + row_bias
            board[part, cols] = scores
            tops = scores if tops is None else jnp.maximum(tops, scores)
            before = peak[pair, :, cols]
            now = jnp.maximum(before, jnp.max(scores, axis=0, keepdims=True))
            peak[pair, :, cols] = now
            mass[pair, :, cols] = mass[pair, :, cols] * jnp.exp2(before - now)
        top = jnp.max(tops, axis=1, keepdims=True)
        wide = jnp.broadcast_to(top, (PIECE, 128))
        sums = None
        for j in range(0, length, 128):
            cols = slice(j, j + 128)
            scores = board[part, cols]
            value = jnp.exp2(scores - wide)
            sums = value if sums is None else sums + value
            value = jnp.exp2(scores - peak[pair, :, cols])
            mass[pair, :, cols] = mass[pair, :, cols] + jnp.sum(value, axis=0, keepdims=True)
        return top + jnp.log2(jnp.sum(sums, axis=1, keepdims=True))

    def close(slot, pair):
        total[slot] = total[slot] + peak[pair] + jnp.log2(mass[pair])

    local.wait()
    set_bias(0, lens[0])
    normalise(0)
    spread(0, 1, ring(partner)).wait_recv()
    spread(1, 2, ring(partner)).wait_recv()

    @pl.when(role != 0)
    def _():
        further().start()

    @pl.when(role == 0)
    def _():
        near.wait_recv()

    @pl.when(role != 1)
    def _():
        set_bias(2, lens[1])
        normalise(1)

    base = jnp.where((role == 0) | (role == 3), 2, 0)
    last = jnp.where(role >= 2, 2 - base, base)

    def arrive(slot, k):
        remote(x_hbm.at[0, rows_of(k)], far.at[slot, rows_of(k)], pass_send.at[0, 0], far_recv.at[slot, k], across).wait_recv()

    def passing(slot, k):
        target = jnp.where(even, me + 4, me - 4)
        there = jnp.where(even, slot + 2, slot + 1)
        return remote(far.at[slot, rows_of(k)], far.at[there, rows_of(k)], pass_send.at[slot, k], far_recv.at[there, k], ring(target))

    def hand_on(slot, k):
        arrive(slot, k)
        passing(slot, k).start()

    def tile_rows(tile):
        return pl.ds(pl.multiple_of(tile * ROWS, ROWS), ROWS)

    def take_local(slot, k, stage, h):
        fresh[stage, h * PIECE : (h + 1) * PIECE] = units[slot, rows_of(k)]

    def take_far(slot, k, stage, h):
        fresh[stage, h * PIECE : (h + 1) * PIECE] = unit_rows(far[slot, rows_of(k)])

    own_len = [lens[0, a : a + 1] for a in range(2)]
    is0, is1, is2, is3 = (jnp.full((1, 128), role, jnp.int32) == r for r in range(4))
    pick = lambda v0, v1, v2, v3: jnp.where(is0, v0, jnp.where(is1, v1, jnp.where(is2, v2, v3)))

    def lens_at(slot, a):
        return lens[slot, a : a + 1]

    def soon():
        return (
            pick(own_len[0], lens_at(2, 0), lens_at(1, 0), own_len[1]),
            pick(own_len[1], lens_at(2, 1), lens_at(2, 0), lens_at(2, 1)),
        )

    def later():
        return (
            pick(lens_at(2, 0), lens_at(3, 0), lens_at(3, 0), lens_at(3, 1)),
            pick(lens_at(2, 1), lens_at(3, 1), lens_at(3, 0), lens_at(3, 1)),
        )

    choose = lambda v0, v1, v2, v3: jnp.where(role == 0, v0, jnp.where(role == 1, v1, jnp.where(role == 2, v2, v3)))
    slots = [choose(0, 4, 2, 1), choose(1, 5, 4, 4), choose(4, 6, 5, 5), choose(5, 7, 5, 5)]

    def routes(j, act):
        for i in range(len(PACE)):
            if starts[i] < starts[i + 1]:
                @pl.when(j == i)
                def _():
                    for a, k in routed[starts[i] : starts[i + 1]]:
                        act(a, k)

    def turn(a, k):
        around(a, k).wait_recv()
        bypass(a, k).start()

    def give(src, dst, device):
        return remote(total.at[src], back.at[dst], back_send.at[src], back_recv.at[dst], device)

    early = (
        [],
        [give(4, 2, ring(me + 2)), give(5, 3, ring(me + 2))],
        [give(4, 2, ring(me - 2))],
        [give(4, 3, ring(me - 3))],
    )

    lag = jnp.where(role == 0, chunks, per)

    def step(j, carry):
        @pl.when(j == chunks)
        def _():
            close(0, 8)
            for s in range(2):
                for a in range(2):
                    close(base + a, 2 * s + a)
            for r in range(1, 4):
                @pl.when(role == r)
                def _():
                    for copy in early[r]:
                        copy.start()

        @pl.when(role == 2)
        def _():
            routes(j, lambda a, k: around(a, k).start())

        @pl.when(j < chunks)
        def _():
            @pl.when(role == 1)
            def _():
                hand_on(0, j)
                take_far(0, j, 0, 0)

            @pl.when(role != 1)
            def _():
                take_local(choose(0, 0, 2, 1), j, 0, 0)

            @pl.when(role == 0)
            def _():
                take_local(1, j, 0, 1)

            @pl.when(role != 0)
            def _():
                slot = jnp.where(role == 1, 1, 0)
                hand_on(slot, j)
                take_far(slot, j, 0, 1)

            counts = soon()
            unit(fresh[0], base, 2, [(counts[0], j * PIECE, 0, slots[0]), (counts[1], j * PIECE, 2, slots[1])])

            @pl.when(lax.rem(j, per) == 0)
            def _():
                unit(units[1, tile_rows(j // per)], 0, 1, [(own_len[1], (j + h) * PIECE, 8, 1) for h in range(per)])

        @pl.when((j >= lag) & (j < lag + chunks))
        def _():
            k = j - lag
            late = lax.rem(k, per)

            @pl.when((j == lag) & (role != 0))
            def _():
                further().wait_recv()


            @pl.when(even)
            def _():
                for h in range(2):
                    slot = choose(h, 2 + h, 0, 0)
                    arrive(slot, k)
                    take_far(slot, k, 1, h)

            @pl.when(odd & (late == 0))
            def _():
                for h in range(per):
                    arrive(1, k + h)
                    take_far(1, k + h, 1, h)

            left = jnp.where(late == 0, base, last)
            counts = later()
            unit(
                fresh[1], left, 2,
                [
                    (counts[0], jnp.where(even, k, k - late) * PIECE, jnp.where(even, 4, 4 + 2 * late), slots[2]),
                    (counts[1], jnp.where(even, k, k - late + 1) * PIECE, jnp.where(even, 6, 4 + 2 * late), slots[3]),
                ],
            )

        @pl.when(role == 3)
        def _():
            routes(j - TURN, turn)

        return carry

    lax.fori_loop(0, lag + chunks, step, 0)

    gives = (
        [give(4, 2, ring(me + 2)), give(5, 3, ring(me + 2))],
        [give(6, 4, ring(me - 2)), give(7, 5, ring(me - 2))],
        [give(5, 4, ring(me + 2))],
        [give(5, 5, ring(me + 1))],
    )
    for r in range(4):
        @pl.when(role == r)
        def _():
            for copy in gives[r]:
                copy.start()

    for s in range(2, 4):
        left = last if s == 3 else base
        for a in range(2):
            close(left + a, 2 * s + a)

    @pl.when(role != 1)
    def _():
        for a in range(2):
            give(2 + a, a, ring(partner)).start()

    takes = ([2, 3, 4, 5], [0, 1], [0, 1, 2, 3], [0, 1, 2, 3, 4, 5])
    for r in range(4):
        @pl.when(role == r)
        def _():
            for b in takes[r]:
                give(0, b, ring(partner)).wait_recv()
            for a in range(2):
                whole = total[a]
                for b in takes[r]:
                    if b % 2 == a:
                        whole = whole + back[b]
                out_ref[a : a + 1] = jnp.where(bias[a] == 0.0, whole, 0.0)
            for copy in gives[r] + early[r]:
                copy.wait_send()

    @pl.when(role != 1)
    def _():
        for a in range(2):
            give(2 + a, a, ring(partner)).wait_send()

    spread(0, 1, ring(partner)).wait_send()

    @pl.when(role != 1)
    def _():
        spread(1, 2, ring(partner)).wait_send()

    @pl.when(role == 0)
    def _():
        spread(2, 2, ring(partner)).wait_send()

    @pl.when(role != 0)
    def _():
        further().wait_send()

    @pl.when(role != 0)
    def _():
        near.wait_send()

    def sent(a, pieces):
        for k in pieces:
            piece(x_hbm, a, k, a, ring(partner)).wait_send()

    @pl.when(role == 0)
    def _():
        sent(0, range(chunks))
        sent(1, range(chunks))

    @pl.when(role == 2)
    def _():
        sent(1, range(chunks))
        sent(0, direct[0])
        for a, k in routed:
            around(a, k).wait_send()

    @pl.when(role == 3)
    def _():
        sent(0, range(chunks))
        sent(1, direct[1])

    @pl.when(role == 1)
    def _():
        for k in range(chunks):
            for a in range(2):
                passing(a, k).wait_send()

    @pl.when(odd)
    def _():
        for k in range(chunks):
            passing(0, k).wait_send()

    @pl.when(role == 3)
    def _():
        for a, k in routed:
            bypass(a, k).wait_send()


def solution(mesh):
    n = mesh.shape["cand"]
    detour = DETOUR if mesh.shape["group"] % 2 == 0 else (0, 0)

    def shards(embeddings, lengths):
        answers, length, width = embeddings.shape
        chunks = length // PIECE
        dma = pltpu.SemaphoreType.DMA
        sums = pl.pallas_call(
            functools.partial(kernel, n, detour),
            out_shape=jax.ShapeDtypeStruct((answers, length), jnp.float32),
            in_specs=[
                pl.BlockSpec(memory_space=pl.ANY),
                pl.BlockSpec(memory_space=pltpu.SMEM),
            ],
            out_specs=pl.BlockSpec(memory_space=pltpu.VMEM),
            scratch_shapes=[
                pltpu.VMEM((2, answers, length, width), jnp.bfloat16),
                pltpu.VMEM((4, length, width), jnp.bfloat16),
                pltpu.VMEM((4, length, width), jnp.bfloat16),
                pltpu.VMEM((2, chunks, PIECE, width), jnp.bfloat16),
                pltpu.VMEM((2, ROWS, width), jnp.bfloat16),
                pltpu.VMEM((ROWS, length), jnp.float32),
                pltpu.VMEM((ROWS, length), jnp.float32),
                pltpu.VMEM((4, answers, 128), jnp.int32),
                pltpu.VMEM((4, 1, length), jnp.float32),
                pltpu.VMEM((9, 1, length), jnp.float32),
                pltpu.VMEM((9, 1, length), jnp.float32),
                pltpu.VMEM((8, 1, length), jnp.float32),
                pltpu.VMEM((6, 1, length), jnp.float32),
                dma, dma((2,)), dma((4,)), dma((4,)),
                dma((2, chunks)), dma((4, chunks)), dma((2, chunks)), dma((2, chunks)),
                dma((2, chunks)), dma((2, chunks)), dma((8,)), dma((6,)),
                pltpu.SemaphoreType.REGULAR, pltpu.SemaphoreType.REGULAR,
            ],
            compiler_params=pltpu.CompilerParams(collective_id=0, has_side_effects=True),
            name="consensus",
        )(embeddings, lengths)
        return sums * (math.log(2.0) / (256.0 * (answers - 1 + 4 * answers)))

    return jax.shard_map(
        shards,
        mesh=mesh,
        in_specs=(P(("group", "cand"), None, None), P(("group", "cand"))),
        out_specs=P(("group", "cand"), None),
        check_vma=False,
    )
```

```python
import functools
import math

import jax
import jax.numpy as jnp
from jax import lax
from jax.experimental import pallas as pl
from jax.experimental.pallas import tpu as pltpu
from jax.sharding import PartitionSpec as P

MESH = pl.DeviceIdType.MESH
SCALE = 256.0 * math.log2(math.e)
LOW = -1e30
PIECE = 128
ROWS = 256
WIDE = 256
DETOUR = (3, 3)
PACE = (0, 2, 2, 2, 0, 0, 0, 0)
TURN = 1


def unit_rows(raw):
    values = raw.astype(jnp.float32)
    scale = lax.rsqrt(jnp.sum(values * values, axis=-1, keepdims=True) + 1e-06)
    return (values * scale).astype(jnp.bfloat16)


def kernel(
    n, detour, x_hbm, lens_ref, out_ref,
    raw, units, far, relay, fresh, board_a, board_b, lens, bias, peak, mass, total, back,
    local_sem, near_sems, lens_send, lens_recv, send_sem, far_recv, pass_send, turn_send, relay_recv, relay_send,
    back_send, back_recv, up_sem, down_sem,
):
    length = x_hbm.shape[1]
    chunks = length // PIECE
    per = ROWS // PIECE
    boards = (board_a, board_b)
    group = lax.axis_index("group")
    place = lax.axis_index("cand")
    twin = group + 1 - 2 * lax.rem(group, 2)
    flip = lax.rem(group, 2)
    me = place + flip * (n - 1 - 2 * place)
    role = lax.rem(me, 4)
    core = lax.rem(me, 2)
    partner = me + 1 - 2 * core
    even, odd = role < 2, role >= 2

    def spot(m):
        m = lax.rem(m + n, n)
        return m + flip * (n - 1 - 2 * m)

    def ring(m):
        return (group, spot(m))

    across = (twin, place)
    corner = (twin, spot(jnp.where(even, me + 2, me - 2)))

    for a in range(2):
        lens[0, a : a + 1] = jnp.full((1, 128), lens_ref[a], jnp.int32)

    barrier = pltpu.get_barrier_semaphore()
    quad, quads = me // 4, n // 4
    below, above = quad > 0, quad < quads - 1
    meets = [ring(me - role + lax.rem(role + i, 4)) for i in range(1, 4)] + [across, corner]
    for device in meets:
        pl.semaphore_signal(barrier, inc=1, device_id=device, device_id_type=MESH)

    @pl.when(below)
    def _():
        pl.semaphore_signal(barrier, inc=1, device_id=ring(me - 4), device_id_type=MESH)

    @pl.when(above)
    def _():
        pl.semaphore_signal(barrier, inc=1, device_id=ring(me + 4), device_id_type=MESH)

    local = pltpu.make_async_copy(x_hbm, raw.at[0], local_sem)
    local.start()
    pl.semaphore_wait(barrier, len(meets) + below.astype(jnp.int32) + above.astype(jnp.int32))

    def rise():
        @pl.when(below)
        def _():
            pl.semaphore_wait(up_sem, 1)

        @pl.when(above)
        def _():
            pl.semaphore_signal(up_sem, inc=1, device_id=ring(me + 4), device_id_type=MESH)

    def fall():
        @pl.when(above)
        def _():
            pl.semaphore_wait(down_sem, 1)

        @pl.when(below)
        def _():
            pl.semaphore_signal(down_sem, inc=1, device_id=ring(me - 4), device_id_type=MESH)

    def remote(src, dst, send, recv, device):
        return pltpu.make_async_remote_copy(
            src_ref=src, dst_ref=dst, send_sem=send, recv_sem=recv,
            device_id=device, device_id_type=MESH,
        )

    def rows_of(k):
        return pl.ds(pl.multiple_of(k * PIECE, PIECE), PIECE)

    def spread(i, slot, device):
        return remote(lens.at[0], lens.at[slot], lens_send.at[i], lens_recv.at[slot], device)

    def further():
        target = jnp.where(even, me + 4, me - 4)
        return remote(lens.at[2], lens.at[3], lens_send.at[3], lens_recv.at[3], ring(target))

    def meet_far():
        @pl.when(2 * quad < quads)
        def _():
            rise()
            fall()

        @pl.when(2 * quad >= quads)
        def _():
            fall()
            rise()

    near = remote(x_hbm, raw.at[1], near_sems.at[0], near_sems.at[1], ring(partner))

    def piece(src, a, k, slot, device):
        return remote(src.at[a, rows_of(k)], far.at[slot, rows_of(k)], send_sem.at[a, k], far_recv.at[slot, k], device)

    def around(a, k):
        return remote(x_hbm.at[a, rows_of(k)], relay.at[a, k], turn_send.at[a, k], relay_recv.at[a, k], corner)

    def bypass(a, k):
        return remote(relay.at[a, k], far.at[a, rows_of(k)], relay_send.at[a, k], far_recv.at[a, k], across)

    routed = [(a, k) for k in range(chunks) for a in range(2) if k < detour[a]]
    starts = [min(sum(PACE[:i]), len(routed)) for i in range(len(PACE))] + [len(routed)]
    direct = [[k for k in range(chunks) if (a, k) not in routed] for a in range(2)]

    spread(0, 1, ring(partner)).start()

    @pl.when(odd)
    def _():
        spread(1, 2, ring(me - 2)).start()

    @pl.when(role == 0)
    def _():
        spread(1, 2, ring(me + 2)).start()
        spread(2, 2, ring(me + 3)).start()

    @pl.when(role != 0)
    def _():
        near.start()

    @pl.when(role == 0)
    def _():
        for k in range(chunks):
            for a in range(2):
                piece(x_hbm, a, k, 0, ring(me + 2 + a)).start()

    @pl.when(role == 3)
    def _():
        for k in range(chunks):
            piece(x_hbm, 0, k, 0, ring(me - 2)).start()

    @pl.when(odd)
    def _():
        near.wait_recv()

    @pl.when(role == 2)
    def _():
        for k in range(chunks):
            piece(raw.at[1], 1, k, 1, ring(me - 1)).start()
        for k in direct[0]:
            piece(x_hbm, 0, k, 0, ring(me - 2)).start()

    @pl.when(role == 3)
    def _():
        for k in direct[1]:
            piece(raw.at[1], 1, k, 1, ring(me - 3)).start()

    meet_far()
    lane = lax.broadcasted_iota(jnp.int32, (1, length), 1)
    row = lax.broadcasted_iota(jnp.int32, (PIECE, 128), 0)
    eye = lax.broadcasted_iota(jnp.int32, (PIECE, PIECE), 0) == lax.broadcasted_iota(
        jnp.int32, (PIECE, PIECE), 1
    )
    total[...] = jnp.zeros_like(total)
    peak[...] = jnp.full_like(peak, LOW)
    mass[...] = jnp.zeros_like(mass)

    def set_bias(slot, counts):
        for a in range(2):
            bias[slot + a] = jnp.where(lane < counts[a : a + 1, 0:1], 0.0, LOW)

    def normalise(slot):
        def one(i, carry):
            a, k = i // chunks, lax.rem(i, chunks)
            units[2 * slot + a, rows_of(k)] = unit_rows(raw[slot, a, rows_of(k)])
            return carry

        lax.fori_loop(0, 2 * chunks, one, 0)

    def unit(query, left, count, halves):
        for a in range(count):
            for j in range(0, length, WIDE):
                boards[a][:, j : j + WIDE] = lax.dot_general(
                    query, units[left + a, j : j + WIDE], (((1,), (1,)), ((), ())),
                    preferred_element_type=jnp.float32,
                )
        for h, (counts, first, pair, slot) in enumerate(halves):
            part = slice(h * PIECE, (h + 1) * PIECE)
            row_bias = jnp.where(row + first < counts, 0.0, LOW)
            term = None
            for a in range(count):
                value = soften(boards[a], part, left + a, pair + a, row_bias)
                term = value if term is None else term + value
            cols = pl.ds(pl.multiple_of(first, PIECE), PIECE)
            total[slot, :, cols] = total[slot, :, cols] + jnp.sum(
                jnp.where(eye, jnp.broadcast_to(term, (PIECE, PIECE)), 0.0), axis=0, keepdims=True
            )

    def soften(board, part, left, pair, row_bias):
        tops = None
        for j in range(0, length, 128):
            cols = slice(j, j + 128)
            scores = board[part, cols] * SCALE + bias[left, :, cols] + row_bias
            board[part, cols] = scores
            tops = scores if tops is None else jnp.maximum(tops, scores)
            before = peak[pair, :, cols]
            now = jnp.maximum(before, jnp.max(scores, axis=0, keepdims=True))
            peak[pair, :, cols] = now
            mass[pair, :, cols] = mass[pair, :, cols] * jnp.exp2(before - now)
        top = jnp.max(tops, axis=1, keepdims=True)
        wide = jnp.broadcast_to(top, (PIECE, 128))
        sums = None
        for j in range(0, length, 128):
            cols = slice(j, j + 128)
            scores = board[part, cols]
            value = jnp.exp2(scores - wide)
            sums = value if sums is None else sums + value
            value = jnp.exp2(scores - peak[pair, :, cols])
            mass[pair, :, cols] = mass[pair, :, cols] + jnp.sum(value, axis=0, keepdims=True)
        return top + jnp.log2(jnp.sum(sums, axis=1, keepdims=True))

    def close(slot, pair):
        total[slot] = total[slot] + peak[pair] + jnp.log2(mass[pair])

    local.wait()
    set_bias(0, lens[0])
    normalise(0)
    spread(0, 1, ring(partner)).wait_recv()
    spread(1, 2, ring(partner)).wait_recv()

    @pl.when(role != 0)
    def _():
        further().start()

    @pl.when(role == 0)
    def _():
        near.wait_recv()

    @pl.when(role != 1)
    def _():
        set_bias(2, lens[1])
        normalise(1)

    base = jnp.where((role == 0) | (role == 3), 2, 0)
    last = jnp.where(role >= 2, 2 - base, base)

    def arrive(slot, k):
        remote(x_hbm.at[0, rows_of(k)], far.at[slot, rows_of(k)], pass_send.at[0, 0], far_recv.at[slot, k], across).wait_recv()

    def passing(slot, k):
        target = jnp.where(even, me + 4, me - 4)
        there = jnp.where(even, slot + 2, slot + 1)
        return remote(far.at[slot, rows_of(k)], far.at[there, rows_of(k)], pass_send.at[slot, k], far_recv.at[there, k], ring(target))

    def hand_on(slot, k):
        arrive(slot, k)
        passing(slot, k).start()

    def tile_rows(tile):
        return pl.ds(pl.multiple_of(tile * ROWS, ROWS), ROWS)

    def take_local(slot, k, stage, h):
        fresh[stage, h * PIECE : (h + 1) * PIECE] = units[slot, rows_of(k)]

    def take_far(slot, k, stage, h):
        fresh[stage, h * PIECE : (h + 1) * PIECE] = unit_rows(far[slot, rows_of(k)])

    own_len = [lens[0, a : a + 1] for a in range(2)]
    is0, is1, is2, is3 = (jnp.full((1, 128), role, jnp.int32) == r for r in range(4))
    pick = lambda v0, v1, v2, v3: jnp.where(is0, v0, jnp.where(is1, v1, jnp.where(is2, v2, v3)))

    def lens_at(slot, a):
        return lens[slot, a : a + 1]

    def soon():
        return (
            pick(own_len[0], lens_at(2, 0), lens_at(1, 0), own_len[1]),
            pick(own_len[1], lens_at(2, 1), lens_at(2, 0), lens_at(2, 1)),
        )

    def later():
        return (
            pick(lens_at(2, 0), lens_at(3, 0), lens_at(3, 0), lens_at(3, 1)),
            pick(lens_at(2, 1), lens_at(3, 1), lens_at(3, 0), lens_at(3, 1)),
        )

    choose = lambda v0, v1, v2, v3: jnp.where(role == 0, v0, jnp.where(role == 1, v1, jnp.where(role == 2, v2, v3)))
    slots = [choose(0, 4, 2, 1), choose(1, 5, 4, 4), choose(4, 6, 5, 5), choose(5, 7, 5, 5)]

    def routes(j, act):
        for i in range(len(PACE)):
            if starts[i] < starts[i + 1]:
                @pl.when(j == i)
                def _():
                    for a, k in routed[starts[i] : starts[i + 1]]:
                        act(a, k)

    def turn(a, k):
        around(a, k).wait_recv()
        bypass(a, k).start()

    lag = jnp.where(role == 0, chunks, per)

    def step(j, carry):
        @pl.when(j == chunks)
        def _():
            close(0, 8)
            for s in range(2):
                for a in range(2):
                    close(base + a, 2 * s + a)

        @pl.when(role == 2)
        def _():
            routes(j, lambda a, k: around(a, k).start())

        @pl.when(j < chunks)
        def _():
            @pl.when(role == 1)
            def _():
                hand_on(0, j)
                take_far(0, j, 0, 0)

            @pl.when(role != 1)
            def _():
                take_local(choose(0, 0, 2, 1), j, 0, 0)

            @pl.when(role == 0)
            def _():
                take_local(1, j, 0, 1)

            @pl.when(role != 0)
            def _():
                slot = jnp.where(role == 1, 1, 0)
                hand_on(slot, j)
                take_far(slot, j, 0, 1)

            counts = soon()
            unit(fresh[0], base, 2, [(counts[0], j * PIECE, 0, slots[0]), (counts[1], j * PIECE, 2, slots[1])])

            @pl.when(lax.rem(j, per) == 0)
            def _():
                unit(units[1, tile_rows(j // per)], 0, 1, [(own_len[1], (j + h) * PIECE, 8, 1) for h in range(per)])

        @pl.when((j >= lag) & (j < lag + chunks))
        def _():
            k = j - lag
            late = lax.rem(k, per)

            @pl.when((j == lag) & (role != 0))
            def _():
                further().wait_recv()


            @pl.when(even)
            def _():
                for h in range(2):
                    slot = choose(h, 2 + h, 0, 0)
                    arrive(slot, k)
                    take_far(slot, k, 1, h)

            @pl.when(odd & (late == 0))
            def _():
                for h in range(per):
                    arrive(1, k + h)
                    take_far(1, k + h, 1, h)

            left = jnp.where(late == 0, base, last)
            counts = later()
            unit(
                fresh[1], left, 2,
                [
                    (counts[0], jnp.where(even, k, k - late) * PIECE, jnp.where(even, 4, 4 + 2 * late), slots[2]),
                    (counts[1], jnp.where(even, k, k - late + 1) * PIECE, jnp.where(even, 6, 4 + 2 * late), slots[3]),
                ],
            )

        @pl.when(role == 3)
        def _():
            routes(j - TURN, turn)

        return carry

    lax.fori_loop(0, lag + chunks, step, 0)

    def give(src, dst, device):
        return remote(total.at[src], back.at[dst], back_send.at[src], back_recv.at[dst], device)

    gives = (
        [give(4, 2, ring(me + 2)), give(5, 3, ring(me + 2))],
        [give(6, 4, ring(me - 2)), give(7, 5, ring(me - 2)), give(4, 2, ring(me + 2)), give(5, 3, ring(me + 2))],
        [give(5, 4, ring(me + 2)), give(4, 2, ring(me - 2))],
        [give(5, 5, ring(me + 1)), give(4, 3, ring(me - 3))],
    )
    for r in range(4):
        @pl.when(role == r)
        def _():
            for copy in gives[r]:
                copy.start()

    for s in range(2, 4):
        left = last if s == 3 else base
        for a in range(2):
            close(left + a, 2 * s + a)

    @pl.when(role != 1)
    def _():
        for a in range(2):
            give(2 + a, a, ring(partner)).start()

    takes = ([2, 3, 4, 5], [0, 1], [0, 1, 2, 3], [0, 1, 2, 3, 4, 5])
    for r in range(4):
        @pl.when(role == r)
        def _():
            for b in takes[r]:
                give(0, b, ring(partner)).wait_recv()
            for a in range(2):
                whole = total[a]
                for b in takes[r]:
                    if b % 2 == a:
                        whole = whole + back[b]
                out_ref[a : a + 1] = jnp.where(bias[a] == 0.0, whole, 0.0)
            for copy in gives[r]:
                copy.wait_send()

    @pl.when(role != 1)
    def _():
        for a in range(2):
            give(2 + a, a, ring(partner)).wait_send()

    spread(0, 1, ring(partner)).wait_send()

    @pl.when(role != 1)
    def _():
        spread(1, 2, ring(partner)).wait_send()

    @pl.when(role == 0)
    def _():
        spread(2, 2, ring(partner)).wait_send()

    @pl.when(role != 0)
    def _():
        further().wait_send()

    @pl.when(role != 0)
    def _():
        near.wait_send()

    def sent(a, pieces):
        for k in pieces:
            piece(x_hbm, a, k, a, ring(partner)).wait_send()

    @pl.when(role == 0)
    def _():
        sent(0, range(chunks))
        sent(1, range(chunks))

    @pl.when(role == 2)
    def _():
        sent(1, range(chunks))
        sent(0, direct[0])
        for a, k in routed:
            around(a, k).wait_send()

    @pl.when(role == 3)
    def _():
        sent(0, range(chunks))
        sent(1, direct[1])

    @pl.when(role == 1)
    def _():
        for k in range(chunks):
            for a in range(2):
                passing(a, k).wait_send()

    @pl.when(odd)
    def _():
        for k in range(chunks):
            passing(0, k).wait_send()

    @pl.when(role == 3)
    def _():
        for a, k in routed:
            bypass(a, k).wait_send()


def solution(mesh):
    n = mesh.shape["cand"]
    detour = DETOUR if mesh.shape["group"] % 2 == 0 else (0, 0)

    def shards(embeddings, lengths):
        answers, length, width = embeddings.shape
        chunks = length // PIECE
        dma = pltpu.SemaphoreType.DMA
        sums = pl.pallas_call(
            functools.partial(kernel, n, detour),
            out_shape=jax.ShapeDtypeStruct((answers, length), jnp.float32),
            in_specs=[
                pl.BlockSpec(memory_space=pl.ANY),
                pl.BlockSpec(memory_space=pltpu.SMEM),
            ],
            out_specs=pl.BlockSpec(memory_space=pltpu.VMEM),
            scratch_shapes=[
                pltpu.VMEM((2, answers, length, width), jnp.bfloat16),
                pltpu.VMEM((4, length, width), jnp.bfloat16),
                pltpu.VMEM((4, length, width), jnp.bfloat16),
                pltpu.VMEM((2, chunks, PIECE, width), jnp.bfloat16),
                pltpu.VMEM((2, ROWS, width), jnp.bfloat16),
                pltpu.VMEM((ROWS, length), jnp.float32),
                pltpu.VMEM((ROWS, length), jnp.float32),
                pltpu.VMEM((4, answers, 128), jnp.int32),
                pltpu.VMEM((4, 1, length), jnp.float32),
                pltpu.VMEM((9, 1, length), jnp.float32),
                pltpu.VMEM((9, 1, length), jnp.float32),
                pltpu.VMEM((8, 1, length), jnp.float32),
                pltpu.VMEM((6, 1, length), jnp.float32),
                dma, dma((2,)), dma((4,)), dma((4,)),
                dma((2, chunks)), dma((4, chunks)), dma((2, chunks)), dma((2, chunks)),
                dma((2, chunks)), dma((2, chunks)), dma((8,)), dma((6,)),
                pltpu.SemaphoreType.REGULAR, pltpu.SemaphoreType.REGULAR,
            ],
            compiler_params=pltpu.CompilerParams(collective_id=0, has_side_effects=True),
            name="consensus",
        )(embeddings, lengths)
        return sums * (math.log(2.0) / (256.0 * (answers - 1 + 4 * answers)))

    return jax.shard_map(
        shards,
        mesh=mesh,
        in_specs=(P(("group", "cand"), None, None), P(("group", "cand"))),
        out_specs=P(("group", "cand"), None),
        check_vma=False,
    )
```
